128 devices in a mesh: expert: 16 (over z, x), wshard: 8 (over y, core).
Axes of the slice: x: 4, y: 4, z: 4, core: 2. Of those that a mesh axis runs over, the one named last changes fastest.
Arguments:
- inputs: float32 [128, 197, 768], P(('expert', 'wshard')), may hold values from -6 to 6
- routes: int32 [2, 128, 197, 2], P(None, ('expert', 'wshard')), may hold values from 0 to 15, all different within a row; in each aligned block of 197 rows (0 to 196, 197 to 393, ..., all dimensions but the last counted through in order) at most 25 rows name the same one
- first_gain: bfloat16 [2, 768], P(None, 'wshard'), may hold values from 0.5 to 1.5
- first_bias: bfloat16 [2, 768], P(None, 'wshard'), may hold values from -3 to 3
- qkv_weight: bfloat16 [2, 768, 2304], P(None, 'wshard'), may hold values from -0.21875 to 0.21875
- proj_weight: bfloat16 [2, 768, 768], P(None, 'wshard'), may hold values from -0.75 to 0.75
- second_gain: bfloat16 [2, 768], P(None, 'wshard'), may hold values from 0.5 to 1.5
- second_bias: bfloat16 [2, 768], P(None, 'wshard'), may hold values from -3 to 3
- router_weight: bfloat16 [2, 768, 16], P(None, 'wshard'), may hold values from -0.4375 to 0.4375
- hidden_weight: bfloat16 [2, 16, 768, 3072], P(None, 'expert', None, 'wshard'), may hold values from -0.21875 to 0.21875
- output_weight: bfloat16 [2, 16, 3072, 768], P(None, 'expert', 'wshard'), may hold values from -0.875 to 0.875
- cotangent: float32 [128, 197, 768], P(('expert', 'wshard')), may hold values from -6 to 6
Outputs:
- outputs: float32 [128, 197, 768], P(('expert', 'wshard'))
- input_grad: float32 [128, 197, 768], P(('expert', 'wshard'))
- first_gain_grad: float32 [2, 768], P(None, 'wshard')
- first_bias_grad: float32 [2, 768], P(None, 'wshard')
- qkv_weight_grad: float32 [2, 768, 2304], P(None, 'wshard')
- proj_weight_grad: float32 [2, 768, 768], P(None, 'wshard')
- second_gain_grad: float32 [2, 768], P(None, 'wshard')
- second_bias_grad: float32 [2, 768], P(None, 'wshard')
- router_weight_grad: float32 [2, 768, 16], P(None, 'wshard')
- hidden_weight_grad: float32 [2, 16, 768, 3072], P(None, 'expert', None, 'wshard')
- output_weight_grad: float32 [2, 16, 3072, 768], P(None, 'expert', 'wshard')
The draws below stay inside these ranges and needn't reach their ends.
Inputs may be any that keep to these rules, and one draw needn't show every extreme that they name: `routes`: each token names two different experts. In each layer the tokens of one image name any one expert at most 25 times over both choices, and that many somewhere.
All inputs are finite; a program needn't handle non-finite values.
Results may differ from the reference program's by a relative error of at most 0.035.
Values may be sent and summed in bfloat16 or wider, within the bound.
No kernel may reach another device: no remote copies, remote signals or barrier semaphores. Data moves between devices by JAX's collectives and lax.ppermute only.
A program may use at most 192 MiB of HBM per device.

```python
import math
import jax
import jax.numpy as jnp
import numpy as np
from jax import lax

D = 768
HEADS = 12
HD = 64
HID = 3072
SEQ = 197
LAYERS = 2
CAP = 25
EXPERTS = 16
IMAGES = 128


def level_of(rng, dims, shards, smallest, largest):
    def one(position, blocks):
        draws = jax.random.uniform(jax.random.fold_in(jax.random.fold_in(rng, 6), position), (blocks,), jnp.float32, smallest / len(shards), largest / len(shards))
        return jnp.repeat(jnp.exp(draws), dims[position] // blocks).reshape((-1,) + (1,) * (len(dims) - position - 1))

    level = one(*shards[0])
    for cut in shards[1:]:
        level = level * one(*cut)
    return level


def routed_block(key, own, number, rows, amount, top, most, skew):
    ranking = jax.random.permutation(key, amount)
    crowded, common = shares(amount, rows * top, most, skew, True), shares(amount, rows * top, most, skew, False)
    places = jnp.arange(amount)

    def named(lengths, rotation):
        used = int((lengths > 0).sum())
        fixed = max(1, used // 4)
        passed = fixed + (places - fixed + rotation * (used - fixed)) % max(1, amount - fixed)
        return jnp.zeros((amount,), jnp.int32).at[ranking[jnp.where(places < fixed, places, passed)]].set(jnp.asarray(lengths, jnp.int32))

    lengths = jnp.where(number % 4 == 0, named(crowded, number // 4), named(common, number - number // 4 - 1))
    mixed = jax.random.permutation(jax.random.fold_in(own, 3), amount)
    giver, taker = mixed[0:amount // 2 * 2:2], mixed[1:amount // 2 * 2:2]
    slack = jnp.minimum(lengths[giver] - 1, most - lengths[taker]) // 2
    slack = jnp.where((giver == ranking[0]) | (taker == ranking[0]) | (lengths[taker] == 0), 0, jnp.maximum(slack, 0))
    passed = jax.random.randint(jax.random.fold_in(own, 4), (amount // 2,), 0, 1 << 20) % (slack + 1)
    lengths = lengths.at[giver].add(-passed).at[taker].add(passed)
    members = jnp.searchsorted(jnp.cumsum(lengths), jnp.arange(rows * top), side="right").astype(jnp.int32)
    table = members.reshape(top, rows).T
    table = table[jax.random.permutation(jax.random.fold_in(own, 1), rows)]
    rotation = jax.random.randint(jax.random.fold_in(own, 2), (rows, 1), 0, top)
    return jnp.take_along_axis(table, (jnp.arange(top)[None, :] + rotation) % top, axis=1)


def shares(amount, total, limit, slope, full):
    weights = [(1 << 20) // math.isqrt(standing ** slope) + 1 for standing in range(1, amount + 1)]
    largest = limit if full else min(limit, max(-(-total // amount), total * weights[0] // sum(weights)))
    least = 1 if total - largest >= amount - 1 else 0
    holding, spare = [largest] + [least] * (amount - 1), total - largest - least * (amount - 1)
    while spare > 0:
        movable = [i for i in range(1, amount) if holding[i] < largest] or [i for i in range(1, amount) if holding[i] < limit]
        mass, remaining = sum([weights[i] for i in movable]), spare
        for i in movable:
            extra = min(limit - holding[i], max(1, remaining * weights[i] // mass), spare)
            holding[i] = holding[i] + extra
            spare = spare - extra
    return np.array(holding)


def scatter_about(key, extent, scale, limit, pieces=(), held_as=jnp.bfloat16):
    loudness = level_of(key, extent, pieces, -0.22, 0.18) if pieces else 1.0
    drawn = jax.random.normal(key, extent, jnp.float32) * scale * loudness
    return jnp.minimum(jnp.maximum(drawn, -limit), limit).astype(held_as)


def setup_inputs(seed: int = 0) -> dict:
    streams_of = jax.random.split(jax.random.key(seed), 13)
    inputs = scatter_about(streams_of[0], (IMAGES, SEQ, D), 1.0, 6.0, ((0, 128),), jnp.float32)
    routes_keys = jax.random.split(jax.random.fold_in(streams_of[1], 1), LAYERS * IMAGES * SEQ // SEQ)
    routes_turns = jax.random.permutation(jax.random.fold_in(streams_of[1], 3), LAYERS * IMAGES * SEQ // SEQ)
    routes = jax.vmap(lambda own, number: routed_block(jax.random.fold_in(streams_of[1], 2), own, number, SEQ, EXPERTS, 2, CAP, 2))(routes_keys, routes_turns).reshape((LAYERS, IMAGES, SEQ, 2))
    first_gain = jnp.clip(1.0 + 0.1 * jax.random.normal(streams_of[2], (LAYERS, D), jnp.float32), 0.5, 1.5).astype(jnp.bfloat16)
    first_bias = scatter_about(streams_of[3], (LAYERS, D), 0.5, 3.0, ((1, 8),))
    qkv_weight = scatter_about(streams_of[4], (LAYERS, D, 3 * D), D ** -0.5, 0.21875, ((1, 8),))
    proj_weight = scatter_about(streams_of[5], (LAYERS, D, D), (D // 12) ** -0.5, 0.75, ((1, 8),))
    second_gain = jnp.clip(1.0 + 0.1 * jax.random.normal(streams_of[6], (LAYERS, D), jnp.float32), 0.5, 1.5).astype(jnp.bfloat16)
    second_bias = scatter_about(streams_of[7], (LAYERS, D), 0.5, 3.0, ((1, 8),))
    router_weight = scatter_about(streams_of[8], (LAYERS, D, EXPERTS), (D // 4) ** -0.5, 0.4375, ((1, 8),))
    hidden_weight = scatter_about(streams_of[9], (LAYERS, EXPERTS, D, HID), D ** -0.5, 0.21875, ((1, 16), (3, 8)))
    output_weight = scatter_about(streams_of[10], (LAYERS, EXPERTS, HID, D), (max(HID // 64, 1)) ** -0.5, 0.875, ((1, 16), (2, 8)))
    cotangent = scatter_about(streams_of[11], (IMAGES, SEQ, D), 1.0, 6.0, ((0, 128),), jnp.float32)
    return dict(inputs=inputs, routes=routes, first_gain=first_gain, first_bias=first_bias, qkv_weight=qkv_weight, proj_weight=proj_weight, second_gain=second_gain, second_bias=second_bias, router_weight=router_weight, hidden_weight=hidden_weight, output_weight=output_weight, cotangent=cotangent)


EPSILON = 1e-06
ROOT_HALF = 0.7071067811865476
INV_ROOT_TAU = 0.3989422804014327

def widen(value):
    return lax.optimization_barrier(value).astype(jnp.float32)

def standardize(rows):
    center = lax.optimization_barrier(jnp.mean(rows, axis=-1, keepdims=True))
    shifted = rows - center
    variance = lax.optimization_barrier(jnp.mean(shifted * shifted, axis=-1, keepdims=True))
    inverse = lax.rsqrt(variance + EPSILON)
    return (shifted * inverse, inverse)

def norm_backward(grad_in, normed, inverse, gain):
    scaled = grad_in * gain.astype(jnp.float32)
    first = lax.optimization_barrier(jnp.mean(scaled, axis=-1, keepdims=True))
    second = lax.optimization_barrier(jnp.mean(scaled * normed, axis=-1, keepdims=True))
    return inverse * (scaled - first - normed * second)

def gelu_value(pre):
    return 0.5 * pre * (1.0 + jax.scipy.special.erf(pre * ROOT_HALF))

def gelu_slope(pre):
    return 0.5 * (1.0 + jax.scipy.special.erf(pre * ROOT_HALF)) + pre * jnp.exp(-0.5 * pre * pre) * INV_ROOT_TAU

def slot_table(flat_routes, count):
    onehot = (flat_routes[..., None] == jnp.arange(count, dtype=jnp.int32)).astype(jnp.int32)
    before = jnp.cumsum(onehot, axis=-2) - onehot
    return lax.optimization_barrier(jnp.sum(before * onehot, axis=-1)).astype(jnp.int32)

def expert_forward(operands):
    rows, hidden, output = operands
    flat_rows = rows.reshape(-1, rows.shape[-1])
    pre = jnp.dot(flat_rows, hidden, preferred_element_type=jnp.float32)
    act = gelu_value(pre).astype(jnp.bfloat16)
    result = jnp.dot(act, output, preferred_element_type=jnp.float32).astype(jnp.bfloat16)
    return result.reshape(rows.shape)

def expert_backward(operands):
    rows, grads, hidden, output = operands
    flat_rows = rows.reshape(-1, rows.shape[-1])
    flat_grads = grads.reshape(-1, rows.shape[-1])
    pre = jnp.dot(flat_rows, hidden, preferred_element_type=jnp.float32)
    act = gelu_value(pre).astype(jnp.bfloat16)
    act_grad = jnp.dot(flat_grads, output.T, preferred_element_type=jnp.float32)
    output_part = jnp.dot(act.T, flat_grads, preferred_element_type=jnp.float32)
    pre_grad = (act_grad * gelu_slope(pre)).astype(jnp.bfloat16)
    hidden_part = jnp.dot(flat_rows.T, pre_grad, preferred_element_type=jnp.float32)
    row_grad = jnp.dot(pre_grad, hidden.T, preferred_element_type=jnp.float32).astype(jnp.bfloat16)
    return (hidden_part, output_part, row_grad.reshape(rows.shape))

def reference(inputs, routes, first_gain, first_bias, qkv_weight, proj_weight, second_gain, second_bias, router_weight, hidden_weight, output_weight, cotangent):
    images, length, width = inputs.shape
    scale = 1.0 / math.sqrt(HD)
    image_index = jnp.arange(images, dtype=jnp.int32)[:, None]
    expert_ids = jnp.arange(EXPERTS, dtype=jnp.int32)
    state = inputs
    saved = []
    for layer in range(LAYERS):
        gain_one = first_gain[layer].astype(jnp.float32)
        bias_one = first_bias[layer].astype(jnp.float32)
        gain_two = second_gain[layer].astype(jnp.float32)
        bias_two = second_bias[layer].astype(jnp.float32)
        normed_one, inverse_one = standardize(state)
        attn_in = (normed_one * gain_one + bias_one).astype(jnp.bfloat16)
        qkv = jnp.dot(attn_in, qkv_weight[layer], preferred_element_type=jnp.float32).astype(jnp.bfloat16)
        query = qkv[..., :width].reshape(images, length, HEADS, HD)
        keys = qkv[..., width:2 * width].reshape(images, length, HEADS, HD)
        values = qkv[..., 2 * width:].reshape(images, length, HEADS, HD)
        scores = jnp.einsum('ishd,ithd->ihst', widen(query), widen(keys)) * scale
        log_total = jnp.log(lax.optimization_barrier(jnp.sum(jnp.exp(scores), axis=-1, keepdims=True)))
        probs_low = jnp.exp(scores - log_total).astype(jnp.bfloat16)
        mixed = jnp.einsum('ihst,ithd->ishd', widen(probs_low), widen(values))
        mixed = mixed.reshape(images, length, width).astype(jnp.bfloat16)
        middle = state + jnp.dot(mixed, proj_weight[layer], preferred_element_type=jnp.float32)
        normed_two, inverse_two = standardize(middle)
        moe_in = (normed_two * gain_two + bias_two).astype(jnp.bfloat16)
        logits = jnp.dot(moe_in, router_weight[layer], preferred_element_type=jnp.float32)
        raised = jnp.exp(logits)
        router_probs = raised / lax.optimization_barrier(jnp.sum(raised, axis=-1, keepdims=True))
        chosen = routes[layer]
        choice_mask = (chosen[..., None] == expert_ids).astype(jnp.float32)
        gates = lax.optimization_barrier(jnp.sum(choice_mask * router_probs[:, :, None, :], axis=-1))
        flat = chosen.reshape(images, 2 * length)
        slots = slot_table(flat, EXPERTS)
        buffer = jnp.zeros((EXPERTS, images, CAP, width), jnp.bfloat16)
        buffer = buffer.at[flat, image_index, slots].set(jnp.repeat(moe_in, 2, axis=1))
        expert_out = lax.map(expert_forward, (buffer, hidden_weight[layer], output_weight[layer]))
        picked = expert_out[flat, image_index, slots].reshape(images, length, 2, width)
        state = middle + lax.optimization_barrier(jnp.sum(gates[..., None] * widen(picked), axis=2))
        saved.append((normed_one, inverse_one, attn_in, query, keys, values, log_total, mixed, normed_two, inverse_two, moe_in, router_probs, choice_mask, gates, flat, slots, buffer, picked))
    outputs = state
    grad = cotangent
    grads_out = []
    for layer in reversed(range(LAYERS)):
        normed_one, inverse_one, attn_in, query, keys, values, log_total, mixed, normed_two, inverse_two, moe_in, router_probs, choice_mask, gates, flat, slots, buffer, picked = saved[layer]
        gate_grad = lax.optimization_barrier(jnp.sum(grad[:, :, None, :] * widen(picked), axis=-1))
        routed_grad = (gates[..., None] * grad[:, :, None, :]).astype(jnp.bfloat16).reshape(images, 2 * length, width)
        grad_buffer = jnp.zeros((EXPERTS, images, CAP, width), jnp.bfloat16)
        grad_buffer = grad_buffer.at[flat, image_index, slots].set(routed_grad)
        hidden_grad, output_grad, row_grads = lax.map(expert_backward, (buffer, grad_buffer, hidden_weight[layer], output_weight[layer]))
        back = row_grads[flat, image_index, slots].reshape(images, length, 2, width)
        prob_grad = lax.optimization_barrier(jnp.sum(choice_mask * gate_grad[..., None], axis=2))
        logit_grad = router_probs * (prob_grad - lax.optimization_barrier(jnp.sum(router_probs * prob_grad, axis=-1, keepdims=True)))
        logit_grad = logit_grad.astype(jnp.bfloat16)
        router_grad = jnp.dot(moe_in.reshape(-1, width).T, logit_grad.reshape(-1, EXPERTS), preferred_element_type=jnp.float32)
        moe_in_grad = lax.optimization_barrier(jnp.sum(widen(back), axis=2)) + jnp.dot(logit_grad, router_weight[layer].T, preferred_element_type=jnp.float32)
        second_gain_grad = lax.optimization_barrier(jnp.sum((moe_in_grad * normed_two).reshape(-1, width), axis=0))
        second_bias_grad = lax.optimization_barrier(jnp.sum(moe_in_grad.reshape(-1, width), axis=0))
        middle_grad = grad + norm_backward(moe_in_grad, normed_two, inverse_two, second_gain[layer])
        middle_low = middle_grad.astype(jnp.bfloat16)
        proj_grad = jnp.dot(mixed.reshape(-1, width).T, middle_low.reshape(-1, width), preferred_element_type=jnp.float32)
        mixed_grad = jnp.dot(middle_low, proj_weight[layer].T, preferred_element_type=jnp.float32).astype(jnp.bfloat16)
        mixed_grad = mixed_grad.reshape(images, length, HEADS, HD)
        scores = jnp.einsum('ishd,ithd->ihst', widen(query), widen(keys)) * scale
        probs = jnp.exp(scores - log_total)
        probs_low = probs.astype(jnp.bfloat16)
        values_grad = jnp.einsum('ihst,ishd->ithd', widen(probs_low), widen(mixed_grad))
        prob_grad_att = jnp.einsum('ishd,ithd->ihst', widen(mixed_grad), widen(values))
        score_grad = probs * (prob_grad_att - lax.optimization_barrier(jnp.sum(probs * prob_grad_att, axis=-1, keepdims=True)))
        score_low = (score_grad * scale).astype(jnp.bfloat16)
        query_grad = jnp.einsum('ihst,ithd->ishd', widen(score_low), widen(keys))
        keys_grad = jnp.einsum('ihst,ishd->ithd', widen(score_low), widen(query))
        qkv_grad = jnp.concatenate([query_grad.reshape(images, length, width), keys_grad.reshape(images, length, width), values_grad.reshape(images, length, width)], axis=-1).astype(jnp.bfloat16)
        qkv_grad_weight = jnp.dot(attn_in.reshape(-1, width).T, qkv_grad.reshape(-1, 3 * width), preferred_element_type=jnp.float32)
        attn_in_grad = jnp.dot(qkv_grad, qkv_weight[layer].T, preferred_element_type=jnp.float32)
        first_gain_grad = lax.optimization_barrier(jnp.sum((attn_in_grad * normed_one).reshape(-1, width), axis=0))
        first_bias_grad = lax.optimization_barrier(jnp.sum(attn_in_grad.reshape(-1, width), axis=0))
        grad = middle_grad + norm_backward(attn_in_grad, normed_one, inverse_one, first_gain[layer])
        grads_out.append((first_gain_grad, first_bias_grad, qkv_grad_weight, proj_grad, second_gain_grad, second_bias_grad, router_grad, hidden_grad, output_grad))
    grads_out = list(reversed(grads_out))
    stacked = [jnp.stack([entry[index] for entry in grads_out]) for index in range(9)]
    return (outputs, grad, stacked[0], stacked[1], stacked[2], stacked[3], stacked[4], stacked[5], stacked[6], stacked[7], stacked[8])
```

```python
import math

import jax
import jax.numpy as jnp
from jax import lax
from jax.experimental import pallas as pl
from jax.experimental.pallas import tpu as pltpu
from jax.sharding import PartitionSpec as P

HEADS = 12
SLOTS = 32
BLOCKS = 8
MISC = 128

EPSILON = 1e-06
ROOT_HALF = 0.7071067811865476
INV_ROOT_TAU = 0.3989422804014327


def standardize(rows):
    center = jnp.mean(rows, axis=-1, keepdims=True)
    shifted = rows - center
    variance = jnp.mean(shifted * shifted, axis=-1, keepdims=True)
    inverse = lax.rsqrt(variance + EPSILON)
    return (shifted * inverse, inverse)


def norm_backward(grad_in, normed, inverse, gain):
    scaled = grad_in * gain.astype(jnp.float32)
    first = jnp.mean(scaled, axis=-1, keepdims=True)
    second = jnp.mean(scaled * normed, axis=-1, keepdims=True)
    return inverse * (scaled - first - normed * second)


def matmul(left, right):
    return jnp.dot(left, right, preferred_element_type=jnp.float32)


def dot_nt(left, right):
    return lax.dot_general(
        left, right, (((1,), (1,)), ((), ())), preferred_element_type=jnp.float32
    )


def dot_tn(left, right):
    return lax.dot_general(
        left, right, (((0,), (0,)), ((), ())), preferred_element_type=jnp.float32
    )


def ffn_forward_kernel(rows_ref, weight_ref, pre_ref, out_ref, total):
    step = pl.program_id(0)
    width = rows_ref.shape[1]
    pre = dot_nt(rows_ref[...], weight_ref[:, :width])
    pre_ref[...] = pre
    act = (0.5 * pre * (1.0 + lax.erf(pre * ROOT_HALF))).astype(jnp.bfloat16)
    part = matmul(act, weight_ref[:, width:])

    @pl.when(step == 0)
    def _():
        total[...] = part

    @pl.when(step > 0)
    def _():
        total[...] += part

    @pl.when(step == pl.num_programs(0) - 1)
    def _():
        out_ref[...] = total[...].astype(out_ref.dtype)


def ffn_forward(rows, weight):
    count, width = rows.shape
    hidden = weight.shape[0]
    block = hidden // BLOCKS
    return pl.pallas_call(
        ffn_forward_kernel,
        grid=(BLOCKS,),
        in_specs=[
            pl.BlockSpec((count, width), lambda j: (0, 0)),
            pl.BlockSpec((block, 2 * width), lambda j: (j, 0)),
        ],
        out_specs=[
            pl.BlockSpec((count, block), lambda j: (0, j)),
            pl.BlockSpec((count, width), lambda j: (0, 0)),
        ],
        out_shape=[
            jax.ShapeDtypeStruct((count, hidden), jnp.float32),
            jax.ShapeDtypeStruct((count, width), jnp.bfloat16),
        ],
        scratch_shapes=[pltpu.VMEM((count, width), jnp.float32)],
        name="ffn_forward",
    )(rows, weight)


def ffn_backward_kernel(rows_ref, grads_ref, pre_ref, weight_ref, weight_grad_ref, out_ref, total):
    step = pl.program_id(0)
    width = rows_ref.shape[1]
    pre = pre_ref[...]
    phi = 0.5 * (1.0 + lax.erf(pre * ROOT_HALF))
    act = (pre * phi).astype(jnp.bfloat16)
    grads = grads_ref[...]
    act_grad = dot_nt(grads, weight_ref[:, width:])
    slope = phi + pre * jnp.exp(-0.5 * pre * pre) * INV_ROOT_TAU
    pre_grad = (act_grad * slope).astype(jnp.bfloat16)
    weight_grad_ref[:, :width] = dot_tn(pre_grad, rows_ref[...]).astype(jnp.bfloat16)
    weight_grad_ref[:, width:] = dot_tn(act, grads).astype(jnp.bfloat16)
    part = matmul(pre_grad, weight_ref[:, :width])

    @pl.when(step == 0)
    def _():
        total[...] = part

    @pl.when(step > 0)
    def _():
        total[...] += part

    @pl.when(step == pl.num_programs(0) - 1)
    def _():
        out_ref[...] = total[...].astype(out_ref.dtype)


def ffn_backward(rows, grads, pre, weight):
    count, width = rows.shape
    hidden = weight.shape[0]
    block = hidden // BLOCKS
    return pl.pallas_call(
        ffn_backward_kernel,
        grid=(BLOCKS,),
        in_specs=[
            pl.BlockSpec((count, width), lambda j: (0, 0)),
            pl.BlockSpec((count, width), lambda j: (0, 0)),
            pl.BlockSpec((count, block), lambda j: (0, j)),
            pl.BlockSpec((block, 2 * width), lambda j: (j, 0)),
        ],
        out_specs=[
            pl.BlockSpec((block, 2 * width), lambda j: (j, 0)),
            pl.BlockSpec((count, width), lambda j: (0, 0)),
        ],
        out_shape=[
            jax.ShapeDtypeStruct((hidden, 2 * width), jnp.bfloat16),
            jax.ShapeDtypeStruct((count, width), jnp.bfloat16),
        ],
        scratch_shapes=[pltpu.VMEM((count, width), jnp.float32)],
        name="ffn_backward",
    )(rows, grads, pre, weight)


def exchange(rows, experts):
    count, width = rows.shape
    moved = lax.all_to_all(
        rows.reshape(experts, count // experts, width),
        "expert",
        split_axis=0,
        concat_axis=0,
        tiled=True,
    )
    return moved.reshape(count, width)


def sum_over_experts(share, experts):
    count, width = share.shape
    parts = lax.all_to_all(
        share.reshape(experts, count // experts, width),
        "expert",
        split_axis=0,
        concat_axis=0,
        tiled=True,
    )
    total = jnp.sum(parts.astype(jnp.float32), axis=0).astype(jnp.bfloat16)
    spread = lax.all_to_all(
        jnp.broadcast_to(total[None], parts.shape),
        "expert",
        split_axis=0,
        concat_axis=0,
        tiled=True,
    )
    return spread.reshape(count, width).astype(jnp.float32)


def routing(chosen, experts):
    length = chosen.shape[0]
    masks = (chosen.T[:, :, None] == jnp.arange(experts, dtype=jnp.int32)).astype(jnp.bfloat16)
    named = masks[0] + masks[1]
    earlier = jnp.tril(jnp.ones((length, length), jnp.bfloat16), -1)
    before = matmul(earlier, named)
    slots = jnp.sum(before[None] * masks.astype(jnp.float32), axis=-1).astype(jnp.int32)
    position = chosen.T * SLOTS + slots
    return (position[:, :, None] == jnp.arange(experts * SLOTS, dtype=jnp.int32)).astype(
        jnp.bfloat16
    )


def unpack_attn(packed, width, experts):
    base = 4 * width
    vectors = packed[:, base + experts : base + experts + 4].T
    return (
        vectors[0],
        vectors[1],
        packed[:, : 3 * width],
        packed[:, 3 * width : base],
        vectors[2],
        vectors[3],
        packed[:, base : base + experts],
    )


def per_device(
    inputs,
    routes,
    first_gain,
    first_bias,
    qkv_weight,
    proj_weight,
    second_gain,
    second_bias,
    router_weight,
    hidden_weight,
    output_weight,
    cotangent,
):
    experts = lax.axis_size("expert")
    state = inputs[0]
    length, width = state.shape
    head_size = width // HEADS
    scale = 1.0 / math.sqrt(head_size)
    attn_pack = [
        jnp.concatenate(
            [
                qkv_weight[layer],
                proj_weight[layer],
                router_weight[layer],
                first_gain[layer][:, None],
                first_bias[layer][:, None],
                second_gain[layer][:, None],
                second_bias[layer][:, None],
                jnp.zeros((qkv_weight.shape[1], MISC - experts - 4), jnp.bfloat16),
            ],
            axis=1,
        )
        for layer in range(routes.shape[0])
    ]
    expert_pack = [
        jnp.concatenate([hidden_weight[layer, 0].T, output_weight[layer, 0]], axis=1)
        for layer in range(routes.shape[0])
    ]
    depth = routes.shape[0]
    expert_ids = jnp.arange(experts, dtype=jnp.int32)
    saved = []
    for layer in range(depth):
        attn_full = lax.all_gather(attn_pack[layer], "wshard", axis=0, tiled=True)
        gathered = unpack_attn(attn_full, width, experts)
        gain_one, bias_one, qkv_full, proj_full, gain_two, bias_two, router_full = gathered
        normed_one, inverse_one = standardize(state)
        attn_in = (normed_one * gain_one.astype(jnp.float32) + bias_one.astype(jnp.float32)).astype(
            jnp.bfloat16
        )
        qkv = matmul(attn_in, qkv_full).astype(jnp.bfloat16)
        query = qkv[:, :width].reshape(length, HEADS, head_size)
        keys = qkv[:, width : 2 * width].reshape(length, HEADS, head_size)
        values = qkv[:, 2 * width :].reshape(length, HEADS, head_size)
        scores = jnp.einsum("shd,thd->hst", query, keys, preferred_element_type=jnp.float32) * scale
        log_total = jnp.log(jnp.sum(jnp.exp(scores), axis=-1, keepdims=True))
        probs_low = jnp.exp(scores - log_total).astype(jnp.bfloat16)
        mixed = jnp.einsum("hst,thd->shd", probs_low, values, preferred_element_type=jnp.float32)
        mixed = mixed.reshape(length, width).astype(jnp.bfloat16)
        middle = state + matmul(mixed, proj_full)
        normed_two, inverse_two = standardize(middle)
        moe_in = (normed_two * gain_two.astype(jnp.float32) + bias_two.astype(jnp.float32)).astype(
            jnp.bfloat16
        )
        logits = matmul(moe_in, router_full)
        raised = jnp.exp(logits)
        router_probs = raised / jnp.sum(raised, axis=-1, keepdims=True)
        chosen = routes[layer, 0]
        choice_mask = (chosen[..., None] == expert_ids).astype(jnp.float32)
        gates = jnp.sum(choice_mask * router_probs[:, None, :], axis=-1)
        select = routing(chosen, experts)
        select_any = select[0] + select[1]
        sent = dot_tn(select_any, moe_in).astype(jnp.bfloat16)
        received = exchange(sent, experts)
        expert_full = lax.all_gather(expert_pack[layer], "wshard", axis=0, tiled=True)
        pre, result = ffn_forward(received, expert_full)
        kept = (received, pre, expert_full)
        returned = exchange(result, experts)
        picked = [matmul(select[k], returned) for k in range(2)]
        state = middle + gates[:, :1] * picked[0] + gates[:, 1:] * picked[1]
        picked = [entry.astype(jnp.bfloat16) for entry in picked]
        saved.append(
            (
                gathered,
                normed_one,
                inverse_one,
                attn_in,
                query,
                keys,
                values,
                log_total,
                mixed,
                normed_two,
                inverse_two,
                moe_in,
                router_probs,
                choice_mask,
                gates,
                select,
                picked,
                kept,
            )
        )
    grad = cotangent[0]
    layer_parts = []
    expert_parts = []
    for layer in reversed(range(depth)):
        (
            gathered,
            normed_one,
            inverse_one,
            attn_in,
            query,
            keys,
            values,
            log_total,
            mixed,
            normed_two,
            inverse_two,
            moe_in,
            router_probs,
            choice_mask,
            gates,
            select,
            picked,
            kept,
        ) = saved[layer]
        gain_one, bias_one, qkv_full, proj_full, gain_two, bias_two, router_full = gathered
        gate_grad = jnp.stack(
            [jnp.sum(grad * picked[k].astype(jnp.float32), axis=-1) for k in range(2)], axis=-1
        )
        routed_grad = [(gates[:, k : k + 1] * grad).astype(jnp.bfloat16) for k in range(2)]
        grad_sent = dot_tn(
            jnp.concatenate([select[0], select[1]], axis=0), jnp.concatenate(routed_grad, axis=0)
        ).astype(jnp.bfloat16)
        grad_received = exchange(grad_sent, experts)
        rows_kept, pre, expert_full = kept
        expert_grad, row_grad = ffn_backward(rows_kept, grad_received, pre, expert_full)
        expert_part = lax.psum_scatter(expert_grad, "wshard", scatter_dimension=0, tiled=True)
        back = matmul(select[0] + select[1], exchange(row_grad, experts))
        prob_grad = jnp.sum(choice_mask * gate_grad[..., None], axis=1)
        logit_grad = router_probs * (
            prob_grad - jnp.sum(router_probs * prob_grad, axis=-1, keepdims=True)
        )
        logit_grad = logit_grad.astype(jnp.bfloat16)
        router_grad = matmul(moe_in.T, logit_grad)
        moe_in_grad = back + matmul(logit_grad, router_full.T)
        second_gain_grad = jnp.sum(moe_in_grad * normed_two, axis=0)
        second_bias_grad = jnp.sum(moe_in_grad, axis=0)
        middle_grad = grad + norm_backward(moe_in_grad, normed_two, inverse_two, gain_two)
        middle_low = middle_grad.astype(jnp.bfloat16)
        proj_grad = matmul(mixed.T, middle_low)
        mixed_grad = (
            matmul(middle_low, proj_full.T).astype(jnp.bfloat16).reshape(length, HEADS, head_size)
        )
        scores = jnp.einsum("shd,thd->hst", query, keys, preferred_element_type=jnp.float32) * scale
        probs = jnp.exp(scores - log_total)
        probs_low = probs.astype(jnp.bfloat16)
        values_grad = jnp.einsum(
            "hst,shd->thd", probs_low, mixed_grad, preferred_element_type=jnp.float32
        )
        prob_grad_att = jnp.einsum(
            "shd,thd->hst", mixed_grad, values, preferred_element_type=jnp.float32
        )
        score_grad = probs * (
            prob_grad_att - jnp.sum(probs * prob_grad_att, axis=-1, keepdims=True)
        )
        score_low = (score_grad * scale).astype(jnp.bfloat16)
        query_grad = jnp.einsum("hst,thd->shd", score_low, keys, preferred_element_type=jnp.float32)
        keys_grad = jnp.einsum("hst,shd->thd", score_low, query, preferred_element_type=jnp.float32)
        qkv_grad = jnp.concatenate(
            [
                query_grad.reshape(length, width),
                keys_grad.reshape(length, width),
                values_grad.reshape(length, width),
            ],
            axis=-1,
        ).astype(jnp.bfloat16)
        qkv_grad_weight = matmul(attn_in.T, qkv_grad)
        attn_in_grad = matmul(qkv_grad, qkv_full.T)
        first_gain_grad = jnp.sum(attn_in_grad * normed_one, axis=0)
        first_bias_grad = jnp.sum(attn_in_grad, axis=0)
        grad = middle_grad + norm_backward(attn_in_grad, normed_one, inverse_one, gain_one)
        vectors = jnp.stack(
            [first_gain_grad, first_bias_grad, second_gain_grad, second_bias_grad], axis=1
        )
        attn_grad = jnp.concatenate(
            [
                qkv_grad_weight.astype(jnp.bfloat16),
                proj_grad.astype(jnp.bfloat16),
                router_grad.astype(jnp.bfloat16),
                vectors.astype(jnp.bfloat16),
                jnp.zeros((width, MISC - experts - 4), jnp.bfloat16),
            ],
            axis=1,
        )
        share = lax.psum_scatter(attn_grad, "wshard", scatter_dimension=0, tiled=True)
        layer_parts.append(unpack_attn(sum_over_experts(share, experts), width, experts))
        expert_parts.append(
            (
                expert_part[:, :width].T.astype(jnp.float32),
                expert_part[:, width:].astype(jnp.float32),
            )
        )
    layer_parts = list(reversed(layer_parts))
    expert_parts = list(reversed(expert_parts))
    stacked = [jnp.stack([entry[index] for entry in layer_parts]) for index in range(7)]
    hidden_grads = jnp.stack([entry[0] for entry in expert_parts])[:, None]
    output_grads = jnp.stack([entry[1] for entry in expert_parts])[:, None]
    return (
        state[None],
        grad[None],
        stacked[0],
        stacked[1],
        stacked[2],
        stacked[3],
        stacked[4],
        stacked[5],
        stacked[6],
        hidden_grads,
        output_grads,
    )


def solution(mesh):
    in_specs = (
        P(("expert", "wshard"), None, None),
        P(None, ("expert", "wshard"), None, None),
        P(None, "wshard"),
        P(None, "wshard"),
        P(None, "wshard", None),
        P(None, "wshard", None),
        P(None, "wshard"),
        P(None, "wshard"),
        P(None, "wshard", None),
        P(None, "expert", None, "wshard"),
        P(None, "expert", "wshard", None),
        P(("expert", "wshard"), None, None),
    )
    out_specs = (
        P(("expert", "wshard"), None, None),
        P(("expert", "wshard"), None, None),
        P(None, "wshard"),
        P(None, "wshard"),
        P(None, "wshard", None),
        P(None, "wshard", None),
        P(None, "wshard"),
        P(None, "wshard"),
        P(None, "wshard", None),
        P(None, "expert", None, "wshard"),
        P(None, "expert", "wshard", None),
    )
    return jax.shard_map(
        per_device, mesh=mesh, in_specs=in_specs, out_specs=out_specs, check_vma=False
    )
```

```python
import math

import jax
import jax.numpy as jnp
from jax import lax
from jax.experimental import pallas as pl
from jax.experimental.pallas import tpu as pltpu
from jax.sharding import PartitionSpec as P

HEADS = 12
SLOTS = 32
BLOCKS = 8
MISC = 128

EPSILON = 1e-06
ROOT_HALF = 0.7071067811865476
INV_ROOT_TAU = 0.3989422804014327


def standardize(rows):
    center = jnp.mean(rows, axis=-1, keepdims=True)
    shifted = rows - center
    variance = jnp.mean(shifted * shifted, axis=-1, keepdims=True)
    inverse = lax.rsqrt(variance + EPSILON)
    return (shifted * inverse, inverse)


def norm_backward(grad_in, normed, inverse, gain):
    scaled = grad_in * gain.astype(jnp.float32)
    first = jnp.mean(scaled, axis=-1, keepdims=True)
    second = jnp.mean(scaled * normed, axis=-1, keepdims=True)
    return inverse * (scaled - first - normed * second)


def matmul(left, right):
    return jnp.dot(left, right, preferred_element_type=jnp.float32)


def dot_nt(left, right):
    return lax.dot_general(
        left, right, (((1,), (1,)), ((), ())), preferred_element_type=jnp.float32
    )


def dot_tn(left, right):
    return lax.dot_general(
        left, right, (((0,), (0,)), ((), ())), preferred_element_type=jnp.float32
    )


def ffn_forward_kernel(rows_ref, weight_ref, pre_ref, out_ref, total):
    step = pl.program_id(0)
    width = rows_ref.shape[1]
    pre = dot_nt(rows_ref[...], weight_ref[:, :width])
    pre_ref[...] = pre
    act = (0.5 * pre * (1.0 + lax.erf(pre * ROOT_HALF))).astype(jnp.bfloat16)
    part = matmul(act, weight_ref[:, width:])

    @pl.when(step == 0)
    def _():
        total[...] = part

    @pl.when(step > 0)
    def _():
        total[...] += part

    @pl.when(step == pl.num_programs(0) - 1)
    def _():
        out_ref[...] = total[...].astype(out_ref.dtype)


def ffn_forward(rows, weight):
    count, width = rows.shape
    hidden = weight.shape[0]
    block = hidden // BLOCKS
    return pl.pallas_call(
        ffn_forward_kernel,
        grid=(BLOCKS,),
        in_specs=[
            pl.BlockSpec((count, width), lambda j: (0, 0)),
            pl.BlockSpec((block, 2 * width), lambda j: (j, 0)),
        ],
        out_specs=[
            pl.BlockSpec((count, block), lambda j: (0, j)),
            pl.BlockSpec((count, width), lambda j: (0, 0)),
        ],
        out_shape=[
            jax.ShapeDtypeStruct((count, hidden), jnp.float32),
            jax.ShapeDtypeStruct((count, width), jnp.bfloat16),
        ],
        scratch_shapes=[pltpu.VMEM((count, width), jnp.float32)],
        name="ffn_forward",
    )(rows, weight)


def ffn_backward_kernel(rows_ref, grads_ref, pre_ref, weight_ref, weight_grad_ref, out_ref, total):
    step = pl.program_id(0)
    width = rows_ref.shape[1]
    pre = pre_ref[...]
    phi = 0.5 * (1.0 + lax.erf(pre * ROOT_HALF))
    act = (pre * phi).astype(jnp.bfloat16)
    grads = grads_ref[...]
    act_grad = dot_nt(grads, weight_ref[:, width:])
    slope = phi + pre * jnp.exp(-0.5 * pre * pre) * INV_ROOT_TAU
    pre_grad = (act_grad * slope).astype(jnp.bfloat16)
    weight_grad_ref[:, :width] = dot_tn(pre_grad, rows_ref[...]).astype(jnp.bfloat16)
    weight_grad_ref[:, width:] = dot_tn(act, grads).astype(jnp.bfloat16)
    part = matmul(pre_grad, weight_ref[:, :width])

    @pl.when(step == 0)
    def _():
        total[...] = part

    @pl.when(step > 0)
    def _():
        total[...] += part

    @pl.when(step == pl.num_programs(0) - 1)
    def _():
        out_ref[...] = total[...].astype(out_ref.dtype)


def ffn_backward(rows, grads, pre, weight):
    count, width = rows.shape
    hidden = weight.shape[0]
    block = hidden // BLOCKS
    return pl.pallas_call(
        ffn_backward_kernel,
        grid=(BLOCKS,),
        in_specs=[
            pl.BlockSpec((count, width), lambda j: (0, 0)),
            pl.BlockSpec((count, width), lambda j: (0, 0)),
            pl.BlockSpec((count, block), lambda j: (0, j)),
            pl.BlockSpec((block, 2 * width), lambda j: (j, 0)),
        ],
        out_specs=[
            pl.BlockSpec((block, 2 * width), lambda j: (j, 0)),
            pl.BlockSpec((count, width), lambda j: (0, 0)),
        ],
        out_shape=[
            jax.ShapeDtypeStruct((hidden, 2 * width), jnp.bfloat16),
            jax.ShapeDtypeStruct((count, width), jnp.bfloat16),
        ],
        scratch_shapes=[pltpu.VMEM((count, width), jnp.float32)],
        name="ffn_backward",
    )(rows, grads, pre, weight)


def exchange(rows, experts):
    count, width = rows.shape
    moved = lax.all_to_all(
        rows.reshape(experts, count // experts, width),
        "expert",
        split_axis=0,
        concat_axis=0,
        tiled=True,
    )
    return moved.reshape(count, width)


def sum_over_experts(share, experts):
    count, width = share.shape
    parts = lax.all_to_all(
        share.reshape(experts, count // experts, width),
        "expert",
        split_axis=0,
        concat_axis=0,
        tiled=True,
    )
    total = jnp.sum(parts.astype(jnp.float32), axis=0).astype(jnp.bfloat16)
    spread = lax.all_to_all(
        jnp.broadcast_to(total[None], parts.shape),
        "expert",
        split_axis=0,
        concat_axis=0,
        tiled=True,
    )
    return spread.reshape(count, width).astype(jnp.float32)


def routing(chosen, experts):
    length = chosen.shape[0]
    masks = (chosen.T[:, :, None] == jnp.arange(experts, dtype=jnp.int32)).astype(jnp.bfloat16)
    named = masks[0] + masks[1]
    earlier = jnp.tril(jnp.ones((length, length), jnp.bfloat16), -1)
    before = matmul(earlier, named)
    slots = jnp.sum(before[None] * masks.astype(jnp.float32), axis=-1).astype(jnp.int32)
    position = chosen.T * SLOTS + slots
    return (position[:, :, None] == jnp.arange(experts * SLOTS, dtype=jnp.int32)).astype(
        jnp.bfloat16
    )


def unpack_attn(packed, width, experts):
    base = 4 * width
    vectors = packed[:, base + experts : base + experts + 4].T
    return (
        vectors[0],
        vectors[1],
        packed[:, : 3 * width],
        packed[:, 3 * width : base],
        vectors[2],
        vectors[3],
        packed[:, base : base + experts],
    )


def per_device(
    inputs,
    routes,
    first_gain,
    first_bias,
    qkv_weight,
    proj_weight,
    second_gain,
    second_bias,
    router_weight,
    hidden_weight,
    output_weight,
    cotangent,
):
    experts = lax.axis_size("expert")
    state = inputs[0]
    length, width = state.shape
    head_size = width // HEADS
    scale = 1.0 / math.sqrt(head_size)
    attn_pack = [
        jnp.concatenate(
            [
                qkv_weight[layer],
                proj_weight[layer],
                router_weight[layer],
                first_gain[layer][:, None],
                first_bias[layer][:, None],
                second_gain[layer][:, None],
                second_bias[layer][:, None],
                jnp.zeros((qkv_weight.shape[1], MISC - experts - 4), jnp.bfloat16),
            ],
            axis=1,
        )
        for layer in range(routes.shape[0])
    ]
    expert_pack = [
        jnp.concatenate([hidden_weight[layer, 0].T, output_weight[layer, 0]], axis=1)
        for layer in range(routes.shape[0])
    ]
    depth = routes.shape[0]
    expert_ids = jnp.arange(experts, dtype=jnp.int32)
    saved = []
    for layer in range(depth):
        attn_full = lax.all_gather(attn_pack[layer], "wshard", axis=0, tiled=True)
        gathered = unpack_attn(attn_full, width, experts)
        gain_one, bias_one, qkv_full, proj_full, gain_two, bias_two, router_full = gathered
        normed_one, inverse_one = standardize(state)
        attn_in = (normed_one * gain_one.astype(jnp.float32) + bias_one.astype(jnp.float32)).astype(
            jnp.bfloat16
        )
        qkv = matmul(attn_in, qkv_full).astype(jnp.bfloat16)
        query = qkv[:, :width].reshape(length, HEADS, head_size)
        keys = qkv[:, width : 2 * width].reshape(length, HEADS, head_size)
        values = qkv[:, 2 * width :].reshape(length, HEADS, head_size)
        scores = jnp.einsum("shd,thd->hst", query, keys, preferred_element_type=jnp.float32) * scale
        log_total = jnp.log(jnp.sum(jnp.exp(scores), axis=-1, keepdims=True))
        probs_low = jnp.exp(scores - log_total).astype(jnp.bfloat16)
        mixed = jnp.einsum("hst,thd->shd", probs_low, values, preferred_element_type=jnp.float32)
        mixed = mixed.reshape(length, width).astype(jnp.bfloat16)
        middle = state + matmul(mixed, proj_full)
        normed_two, inverse_two = standardize(middle)
        moe_in = (normed_two * gain_two.astype(jnp.float32) + bias_two.astype(jnp.float32)).astype(
            jnp.bfloat16
        )
        logits = matmul(moe_in, router_full)
        raised = jnp.exp(logits)
        router_probs = raised / jnp.sum(raised, axis=-1, keepdims=True)
        chosen = routes[layer, 0]
        choice_mask = (chosen[..., None] == expert_ids).astype(jnp.float32)
        gates = jnp.sum(choice_mask * router_probs[:, None, :], axis=-1)
        select = routing(chosen, experts)
        select_any = select[0] + select[1]
        sent = dot_tn(select_any, moe_in).astype(jnp.bfloat16)
        received = exchange(sent, experts)
        expert_full = lax.all_gather(expert_pack[layer], "wshard", axis=0, tiled=True)
        pre, result = ffn_forward(received, expert_full)
        kept = (received, pre, expert_full)
        returned = exchange(result, experts)
        picked = [matmul(select[k], returned) for k in range(2)]
        state = middle + gates[:, :1] * picked[0] + gates[:, 1:] * picked[1]
        picked = [entry.astype(jnp.bfloat16) for entry in picked]
        saved.append(
            (
                gathered,
                normed_one,
                inverse_one,
                attn_in,
                query,
                keys,
                values,
                log_total,
                mixed,
                normed_two,
                inverse_two,
                moe_in,
                router_probs,
                choice_mask,
                gates,
                select,
                picked,
                kept,
            )
        )
    grad = cotangent[0]
    layer_parts = []
    expert_parts = []
    share = None
    for layer in reversed(range(depth)):
        (
            gathered,
            normed_one,
            inverse_one,
            attn_in,
            query,
            keys,
            values,
            log_total,
            mixed,
            normed_two,
            inverse_two,
            moe_in,
            router_probs,
            choice_mask,
            gates,
            select,
            picked,
            kept,
        ) = saved[layer]
        gain_one, bias_one, qkv_full, proj_full, gain_two, bias_two, router_full = gathered
        gate_grad = jnp.stack(
            [jnp.sum(grad * picked[k].astype(jnp.float32), axis=-1) for k in range(2)], axis=-1
        )
        routed_grad = [(gates[:, k : k + 1] * grad).astype(jnp.bfloat16) for k in range(2)]
        grad_sent = dot_tn(
            jnp.concatenate([select[0], select[1]], axis=0), jnp.concatenate(routed_grad, axis=0)
        ).astype(jnp.bfloat16)
        grad_received = exchange(grad_sent, experts)
        rows_kept, pre, expert_full = kept
        expert_grad, row_grad = ffn_backward(rows_kept, grad_received, pre, expert_full)
        if share is not None:
            expert_grad, share = lax.optimization_barrier((expert_grad, share))
        expert_part = lax.psum_scatter(expert_grad, "wshard", scatter_dimension=0, tiled=True)
        back = matmul(select[0] + select[1], exchange(row_grad, experts))
        prob_grad = jnp.sum(choice_mask * gate_grad[..., None], axis=1)
        logit_grad = router_probs * (
            prob_grad - jnp.sum(router_probs * prob_grad, axis=-1, keepdims=True)
        )
        logit_grad = logit_grad.astype(jnp.bfloat16)
        router_grad = matmul(moe_in.T, logit_grad)
        moe_in_grad = back + matmul(logit_grad, router_full.T)
        second_gain_grad = jnp.sum(moe_in_grad * normed_two, axis=0)
        second_bias_grad = jnp.sum(moe_in_grad, axis=0)
        middle_grad = grad + norm_backward(moe_in_grad, normed_two, inverse_two, gain_two)
        middle_low = middle_grad.astype(jnp.bfloat16)
        proj_grad = matmul(mixed.T, middle_low)
        mixed_grad = (
            matmul(middle_low, proj_full.T).astype(jnp.bfloat16).reshape(length, HEADS, head_size)
        )
        scores = jnp.einsum("shd,thd->hst", query, keys, preferred_element_type=jnp.float32) * scale
        probs = jnp.exp(scores - log_total)
        probs_low = probs.astype(jnp.bfloat16)
        values_grad = jnp.einsum(
            "hst,shd->thd", probs_low, mixed_grad, preferred_element_type=jnp.float32
        )
        prob_grad_att = jnp.einsum(
            "shd,thd->hst", mixed_grad, values, preferred_element_type=jnp.float32
        )
        score_grad = probs * (
            prob_grad_att - jnp.sum(probs * prob_grad_att, axis=-1, keepdims=True)
        )
        score_low = (score_grad * scale).astype(jnp.bfloat16)
        query_grad = jnp.einsum("hst,thd->shd", score_low, keys, preferred_element_type=jnp.float32)
        keys_grad = jnp.einsum("hst,shd->thd", score_low, query, preferred_element_type=jnp.float32)
        qkv_grad = jnp.concatenate(
            [
                query_grad.reshape(length, width),
                keys_grad.reshape(length, width),
                values_grad.reshape(length, width),
            ],
            axis=-1,
        ).astype(jnp.bfloat16)
        qkv_grad_weight = matmul(attn_in.T, qkv_grad)
        attn_in_grad = matmul(qkv_grad, qkv_full.T)
        first_gain_grad = jnp.sum(attn_in_grad * normed_one, axis=0)
        first_bias_grad = jnp.sum(attn_in_grad, axis=0)
        grad = middle_grad + norm_backward(attn_in_grad, normed_one, inverse_one, gain_one)
        vectors = jnp.stack(
            [first_gain_grad, first_bias_grad, second_gain_grad, second_bias_grad], axis=1
        )
        attn_grad = jnp.concatenate(
            [
                qkv_grad_weight.astype(jnp.bfloat16),
                proj_grad.astype(jnp.bfloat16),
                router_grad.astype(jnp.bfloat16),
                vectors.astype(jnp.bfloat16),
                jnp.zeros((width, MISC - experts - 4), jnp.bfloat16),
            ],
            axis=1,
        )
        attn_grad, expert_part = lax.optimization_barrier((attn_grad, expert_part))
        if share is not None:
            attn_grad, share = lax.optimization_barrier((attn_grad, share))
            layer_parts.append(unpack_attn(sum_over_experts(share, experts), width, experts))
        share = lax.psum_scatter(attn_grad, "wshard", scatter_dimension=0, tiled=True)
        expert_parts.append(
            (
                expert_part[:, :width].T.astype(jnp.float32),
                expert_part[:, width:].astype(jnp.float32),
            )
        )
    layer_parts.append(unpack_attn(sum_over_experts(share, experts), width, experts))
    layer_parts = list(reversed(layer_parts))
    expert_parts = list(reversed(expert_parts))
    stacked = [jnp.stack([entry[index] for entry in layer_parts]) for index in range(7)]
    hidden_grads = jnp.stack([entry[0] for entry in expert_parts])[:, None]
    output_grads = jnp.stack([entry[1] for entry in expert_parts])[:, None]
    return (
        state[None],
        grad[None],
        stacked[0],
        stacked[1],
        stacked[2],
        stacked[3],
        stacked[4],
        stacked[5],
        stacked[6],
        hidden_grads,
        output_grads,
    )


def solution(mesh):
    in_specs = (
        P(("expert", "wshard"), None, None),
        P(None, ("expert", "wshard"), None, None),
        P(None, "wshard"),
        P(None, "wshard"),
        P(None, "wshard", None),
        P(None, "wshard", None),
        P(None, "wshard"),
        P(None, "wshard"),
        P(None, "wshard", None),
        P(None, "expert", None, "wshard"),
        P(None, "expert", "wshard", None),
        P(("expert", "wshard"), None, None),
    )
    out_specs = (
        P(("expert", "wshard"), None, None),
        P(("expert", "wshard"), None, None),
        P(None, "wshard"),
        P(None, "wshard"),
        P(None, "wshard", None),
        P(None, "wshard", None),
        P(None, "wshard"),
        P(None, "wshard"),
        P(None, "wshard", None),
        P(None, "expert", None, "wshard"),
        P(None, "expert", "wshard", None),
    )
    return jax.shard_map(
        per_device, mesh=mesh, in_specs=in_specs, out_specs=out_specs, check_vma=False
    )
```

```python
import functools
import math

import jax
import jax.numpy as jnp
from jax import lax
from jax.experimental import pallas as pl
from jax.experimental.pallas import tpu as pltpu
from jax.sharding import PartitionSpec as P

HEADS = 12
SLOTS = 32
BLOCKS = 8
MISC = 128

EPSILON = 1e-06
ROOT_HALF = 0.7071067811865476
INV_ROOT_TAU = 0.3989422804014327


def standardize(rows):
    center = jnp.mean(rows, axis=-1, keepdims=True)
    shifted = rows - center
    variance = jnp.mean(shifted * shifted, axis=-1, keepdims=True)
    inverse = lax.rsqrt(variance + EPSILON)
    return (shifted * inverse, inverse)


def norm_backward(grad_in, normed, inverse, gain):
    scaled = grad_in * gain.astype(jnp.float32)
    first = jnp.mean(scaled, axis=-1, keepdims=True)
    second = jnp.mean(scaled * normed, axis=-1, keepdims=True)
    return inverse * (scaled - first - normed * second)


def matmul(left, right):
    return jnp.dot(left, right, preferred_element_type=jnp.float32)


def dot_nt(left, right):
    return lax.dot_general(
        left, right, (((1,), (1,)), ((), ())), preferred_element_type=jnp.float32
    )


def dot_tn(left, right):
    return lax.dot_general(
        left, right, (((0,), (0,)), ((), ())), preferred_element_type=jnp.float32
    )


def ffn_forward_kernel(rows_ref, weight_ref, pre_ref, out_ref, total):
    step = pl.program_id(0)
    width = rows_ref.shape[1]
    pre = dot_nt(rows_ref[...], weight_ref[:, :width])
    pre_ref[...] = pre
    act = (0.5 * pre * (1.0 + lax.erf(pre * ROOT_HALF))).astype(jnp.bfloat16)
    part = matmul(act, weight_ref[:, width:])

    @pl.when(step == 0)
    def _():
        total[...] = part

    @pl.when(step > 0)
    def _():
        total[...] += part

    @pl.when(step == pl.num_programs(0) - 1)
    def _():
        out_ref[...] = total[...].astype(out_ref.dtype)


def ffn_forward(rows, weight):
    count, width = rows.shape
    hidden = weight.shape[0]
    block = hidden // BLOCKS
    return pl.pallas_call(
        ffn_forward_kernel,
        grid=(BLOCKS,),
        in_specs=[
            pl.BlockSpec((count, width), lambda j: (0, 0)),
            pl.BlockSpec((block, 2 * width), lambda j: (j, 0)),
        ],
        out_specs=[
            pl.BlockSpec((count, block), lambda j: (0, j)),
            pl.BlockSpec((count, width), lambda j: (0, 0)),
        ],
        out_shape=[
            jax.ShapeDtypeStruct((count, hidden), jnp.float32),
            jax.ShapeDtypeStruct((count, width), jnp.bfloat16),
        ],
        scratch_shapes=[pltpu.VMEM((count, width), jnp.float32)],
        name="ffn_forward",
    )(rows, weight)


def ffn_backward_kernel(rows_ref, grads_ref, pre_ref, weight_ref, weight_grad_ref, out_ref, total):
    step = pl.program_id(0)
    width = rows_ref.shape[1]
    pre = pre_ref[...]
    phi = 0.5 * (1.0 + lax.erf(pre * ROOT_HALF))
    act = (pre * phi).astype(jnp.bfloat16)
    grads = grads_ref[...]
    act_grad = dot_nt(grads, weight_ref[:, width:])
    slope = phi + pre * jnp.exp(-0.5 * pre * pre) * INV_ROOT_TAU
    pre_grad = (act_grad * slope).astype(jnp.bfloat16)
    weight_grad_ref[:, :width] = dot_tn(pre_grad, rows_ref[...]).astype(jnp.bfloat16)
    weight_grad_ref[:, width:] = dot_tn(act, grads).astype(jnp.bfloat16)
    part = matmul(pre_grad, weight_ref[:, :width])

    @pl.when(step == 0)
    def _():
        total[...] = part

    @pl.when(step > 0)
    def _():
        total[...] += part

    @pl.when(step == pl.num_programs(0) - 1)
    def _():
        out_ref[...] = total[...].astype(out_ref.dtype)


def ffn_backward(rows, grads, pre, weight):
    count, width = rows.shape
    hidden = weight.shape[0]
    block = hidden // BLOCKS
    return pl.pallas_call(
        ffn_backward_kernel,
        grid=(BLOCKS,),
        in_specs=[
            pl.BlockSpec((count, width), lambda j: (0, 0)),
            pl.BlockSpec((count, width), lambda j: (0, 0)),
            pl.BlockSpec((count, block), lambda j: (0, j)),
            pl.BlockSpec((block, 2 * width), lambda j: (j, 0)),
        ],
        out_specs=[
            pl.BlockSpec((block, 2 * width), lambda j: (j, 0)),
            pl.BlockSpec((count, width), lambda j: (0, 0)),
        ],
        out_shape=[
            jax.ShapeDtypeStruct((hidden, 2 * width), jnp.bfloat16),
            jax.ShapeDtypeStruct((count, width), jnp.bfloat16),
        ],
        scratch_shapes=[pltpu.VMEM((count, width), jnp.float32)],
        name="ffn_backward",
    )(rows, grads, pre, weight)


def ffn_both_kernel(rows_ref, grads_ref, weight_ref, weight_grad_ref, out_ref, back_ref, total, back):
    step = pl.program_id(0)
    width = rows_ref.shape[1]
    rows = rows_ref[...]
    grads = grads_ref[...]
    pre = dot_nt(rows, weight_ref[:, :width])
    act_grad = dot_nt(grads, weight_ref[:, width:])
    phi = 0.5 * (1.0 + lax.erf(pre * ROOT_HALF))
    act = (pre * phi).astype(jnp.bfloat16)
    slope = phi + pre * jnp.exp(-0.5 * pre * pre) * INV_ROOT_TAU
    pre_grad = (act_grad * slope).astype(jnp.bfloat16)
    part = matmul(act, weight_ref[:, width:])
    back_part = matmul(pre_grad, weight_ref[:, :width])
    weight_grad_ref[:, :width] = dot_tn(pre_grad, rows).astype(jnp.bfloat16)
    weight_grad_ref[:, width:] = dot_tn(act, grads).astype(jnp.bfloat16)

    @pl.when(step == 0)
    def _():
        total[...] = part
        back[...] = back_part

    @pl.when(step > 0)
    def _():
        total[...] += part
        back[...] += back_part

    @pl.when(step == pl.num_programs(0) - 1)
    def _():
        out_ref[...] = total[...].astype(out_ref.dtype)
        back_ref[...] = back[...].astype(back_ref.dtype)


def ffn_both(pairs, weight):
    count, width = pairs.shape[0], pairs.shape[1] // 2
    hidden = weight.shape[0]
    block = hidden // BLOCKS
    return pl.pallas_call(
        ffn_both_kernel,
        grid=(BLOCKS,),
        in_specs=[
            pl.BlockSpec((count, width), lambda j: (0, 0)),
            pl.BlockSpec((count, width), lambda j: (0, 1)),
            pl.BlockSpec((block, 2 * width), lambda j: (j, 0)),
        ],
        out_specs=[
            pl.BlockSpec((block, 2 * width), lambda j: (j, 0)),
            pl.BlockSpec((count, width), lambda j: (0, 0)),
            pl.BlockSpec((count, width), lambda j: (0, 0)),
        ],
        out_shape=[
            jax.ShapeDtypeStruct((hidden, 2 * width), jnp.bfloat16),
            jax.ShapeDtypeStruct((count, width), jnp.bfloat16),
            jax.ShapeDtypeStruct((count, width), jnp.bfloat16),
        ],
        scratch_shapes=[
            pltpu.VMEM((count, width), jnp.float32),
            pltpu.VMEM((count, width), jnp.float32),
        ],
        name="ffn_both",
    )(pairs, pairs, weight)


def lanes_of(shape):
    return lax.broadcasted_iota(jnp.int32, shape, len(shape) - 1)


def gate_masks(chosen_ref):
    length = chosen_ref.shape[0]
    lane = lanes_of((length, MISC))
    return [chosen_ref[:, k : k + 1] == lane for k in range(2)]


def gates_of(masks, probs):
    return [jnp.sum(jnp.where(mask, probs, 0.0), axis=-1, keepdims=True) for mask in masks]


def small_params(weight_ref, width, experts):
    flipped = weight_ref[:, 4 * width :].astype(jnp.float32).T
    return [flipped[experts + i : experts + i + 1, :] for i in range(4)]


def blocked(count, body):
    lax.fori_loop(0, count, lambda i, carry: (body(i), carry)[1], 0)


def block_of(i, size):
    return pl.ds(pl.multiple_of(i * size, size), size)


def send_grads(place_ref, gates, grad):
    total = None
    for k in range(2):
        part = matmul(place_ref[k], (gates[k] * grad).astype(jnp.bfloat16))
        total = part if total is None else total + part
    return total.astype(jnp.bfloat16)


def attn_forward_kernel(first, last, experts, *refs):
    refs = list(refs)
    if first:
        state_in = refs.pop(0)
    else:
        middle_in, returned_ref, probs_in, chosen_in, pick_ref = refs[:5]
        refs = refs[5:]
    weight_ref, chosen_ref, place_ref = refs[:3]
    refs = refs[3:]
    if last:
        grad_ref = refs.pop(0)
    if not first:
        state_out = refs.pop(0)
    qkv_ref, mixed_ref, middle_ref, probs_ref, sent_ref = refs
    width = weight_ref.shape[0]
    scale = 1.0 / math.sqrt(width // HEADS)
    if first:
        state = state_in[...]
    else:
        gates = gates_of(gate_masks(chosen_in), probs_in[...])
        returned = returned_ref[...]
        state = middle_in[...]
        added = [gates[k] * matmul(pick_ref[k], returned) for k in range(2)]
        state = state + (added[0] + added[1])
        state_out[...] = state
    gain_one, bias_one, gain_two, bias_two = small_params(weight_ref, width, experts)
    normed, _ = standardize(state)
    attn_in = (normed * gain_one + bias_one).astype(jnp.bfloat16)

    def project(i):
        cols = block_of(i, 384)
        qkv_ref[:, cols] = matmul(attn_in, weight_ref[:, cols]).astype(jnp.bfloat16)

    blocked(3 * width // 384, project)
    length = state.shape[0]
    half = lanes_of((length, 128)) < 64

    def heads(i):
        query = qkv_ref[:, block_of(i, 128)]
        keys = qkv_ref[:, pl.ds(pl.multiple_of(width + i * 128, 128), 128)]
        values = qkv_ref[:, pl.ds(pl.multiple_of(2 * width + i * 128, 128), 128)]
        out = []
        for side in range(2):
            mine = half if side == 0 else jnp.logical_not(half)
            scores = dot_nt(jnp.where(mine, query, jnp.zeros_like(query)), keys) * scale
            log_total = jnp.log(jnp.sum(jnp.exp(scores), axis=-1, keepdims=True))
            probs_low = jnp.exp(scores - log_total).astype(jnp.bfloat16)
            out.append(matmul(probs_low, values))
        mixed_ref[:, block_of(i, 128)] = jnp.where(half, out[0], out[1]).astype(jnp.bfloat16)

    blocked(HEADS // 2, heads)
    mixed = mixed_ref[...]

    def combine(i):
        cols = block_of(i, 384)
        middle_ref[:, cols] = matmul(
            mixed, weight_ref[:, pl.ds(pl.multiple_of(3 * width + i * 384, 384), 384)]
        )

    blocked(width // 384, combine)
    middle = state + middle_ref[...]
    middle_ref[...] = middle
    normed_two, _ = standardize(middle)
    moe_in = (normed_two * gain_two + bias_two).astype(jnp.bfloat16)
    logits = matmul(moe_in, weight_ref[:, 4 * width :])
    raised = jnp.where(lanes_of(logits.shape) < experts, jnp.exp(logits), 0.0)
    probs = raised / jnp.sum(raised, axis=-1, keepdims=True)
    probs_ref[...] = probs
    sent = matmul(place_ref[0] + place_ref[1], moe_in)
    sent_ref[:, :width] = sent.astype(jnp.bfloat16)
    if last:
        sent_ref[:, width:] = send_grads(
            place_ref, gates_of(gate_masks(chosen_ref), probs), grad_ref[...]
        )


def whole(count):
    return [pl.BlockSpec(memory_space=pltpu.VMEM) for _ in range(count)]


def attn_forward(source, weight, chosen, place, cotangent):
    first, last = not isinstance(source, tuple), cotangent is not None
    operands = [source] if first else list(source)
    length, width = operands[0].shape
    slots = place.shape[1]
    operands += [weight, chosen, place] + ([cotangent] if last else [])
    outs = [] if first else [jax.ShapeDtypeStruct((length, width), jnp.float32)]
    outs += [
        jax.ShapeDtypeStruct((length, 3 * width), jnp.bfloat16),
        jax.ShapeDtypeStruct((length, width), jnp.bfloat16),
        jax.ShapeDtypeStruct((length, width), jnp.float32),
        jax.ShapeDtypeStruct((length, MISC), jnp.float32),
        jax.ShapeDtypeStruct((slots, width * (2 if last else 1)), jnp.bfloat16),
    ]
    results = pl.pallas_call(
        functools.partial(attn_forward_kernel, first, last, slots // SLOTS),
        in_specs=whole(len(operands)),
        out_specs=whole(len(outs)),
        out_shape=outs,
        name="attn_forward",
    )(*operands)
    return ([source] if first else []) + list(results)


def attn_backward_kernel(last, first, experts, *refs):
    refs = list(refs)
    (
        state_ref,
        middle_ref,
        qkv_ref,
        mixed_ref,
        probs_ref,
        chosen_ref,
        pick_ref,
        returned_ref,
        back_ref,
        grad_ref,
        weight_ref,
    ) = refs[:11]
    refs = refs[11:]
    if not first:
        probs_below, chosen_below, place_below = refs[:3]
        refs = refs[3:]
    grad_out, weight_grad = refs[:2]
    refs = refs[2:]
    if last:
        output_ref = refs.pop(0)
    if not first:
        sent_ref = refs.pop(0)
    mixed_grad_ref, qkv_grad_ref, work_ref = refs
    width = weight_ref.shape[0]
    scale = 1.0 / math.sqrt(width // HEADS)
    grad = grad_ref[...]
    length = grad.shape[0]
    gain_one, bias_one, gain_two, bias_two = small_params(weight_ref, width, experts)
    masks = gate_masks(chosen_ref)
    probs = probs_ref[...]
    middle = middle_ref[...]
    gates = gates_of(masks, probs)
    returned = returned_ref[...]
    picked = [matmul(pick_ref[k], returned) for k in range(2)]
    if last:
        output_ref[...] = middle + (gates[0] * picked[0] + gates[1] * picked[1])
    prob_grad = jnp.zeros_like(probs)
    for k in range(2):
        gate_grad = jnp.sum(grad * picked[k], axis=-1, keepdims=True)
        prob_grad = prob_grad + jnp.where(masks[k], gate_grad, 0.0)
    logit_grad = (
        probs * (prob_grad - jnp.sum(probs * prob_grad, axis=-1, keepdims=True))
    ).astype(jnp.bfloat16)
    normed_two, inverse_two = standardize(middle)
    moe_in = (normed_two * gain_two + bias_two).astype(jnp.bfloat16)
    router_grad = dot_tn(moe_in, logit_grad)
    moe_in_grad = matmul(pick_ref[0] + pick_ref[1], back_ref[...]) + dot_nt(
        logit_grad, weight_ref[:, 4 * width :]
    )
    second_gain_grad = jnp.sum(moe_in_grad * normed_two, axis=0, keepdims=True)
    second_bias_grad = jnp.sum(moe_in_grad, axis=0, keepdims=True)
    middle_grad = grad + norm_backward(moe_in_grad, normed_two, inverse_two, gain_two)
    work_ref[...] = middle_grad
    middle_low = middle_grad.astype(jnp.bfloat16)
    weight_grad[:, 3 * width : 4 * width] = dot_tn(mixed_ref[...], middle_low).astype(jnp.bfloat16)
    mixed_grad_ref[...] = dot_nt(middle_low, weight_ref[:, 3 * width : 4 * width]).astype(
        jnp.bfloat16
    )
    half = lanes_of((length, 128)) < 64

    def heads(i):
        query_cols = block_of(i, 128)
        keys_cols = pl.ds(pl.multiple_of(width + i * 128, 128), 128)
        values_cols = pl.ds(pl.multiple_of(2 * width + i * 128, 128), 128)
        query, keys, values = qkv_ref[:, query_cols], qkv_ref[:, keys_cols], qkv_ref[:, values_cols]
        mixed_grad = mixed_grad_ref[:, query_cols]
        parts = []
        for side in range(2):
            mine = half if side == 0 else jnp.logical_not(half)
            scores = dot_nt(jnp.where(mine, query, jnp.zeros_like(query)), keys) * scale
            log_total = jnp.log(jnp.sum(jnp.exp(scores), axis=-1, keepdims=True))
            probs_att = jnp.exp(scores - log_total)
            prob_grad_att = dot_nt(jnp.where(mine, mixed_grad, jnp.zeros_like(mixed_grad)), values)
            row_total = jnp.sum(probs_att * prob_grad_att, axis=-1, keepdims=True)
            score_low = (probs_att * (prob_grad_att - row_total) * scale).astype(jnp.bfloat16)
            parts.append(
                (
                    matmul(score_low, keys),
                    dot_tn(score_low, query),
                    dot_tn(probs_att.astype(jnp.bfloat16), mixed_grad),
                )
            )
        for cols, index in ((query_cols, 0), (keys_cols, 1), (values_cols, 2)):
            qkv_grad_ref[:, cols] = jnp.where(half, parts[0][index], parts[1][index]).astype(
                jnp.bfloat16
            )

    blocked(HEADS // 2, heads)
    normed_one, inverse_one = standardize(state_ref[...])
    attn_in = (normed_one * gain_one + bias_one).astype(jnp.bfloat16)

    def weights(i):
        cols = block_of(i, 384)
        weight_grad[:, cols] = dot_tn(attn_in, qkv_grad_ref[:, cols]).astype(jnp.bfloat16)

    blocked(3 * width // 384, weights)
    attn_in_grad = dot_nt(qkv_grad_ref[...], weight_ref[:, : 3 * width])
    first_gain_grad = jnp.sum(attn_in_grad * normed_one, axis=0, keepdims=True)
    first_bias_grad = jnp.sum(attn_in_grad, axis=0, keepdims=True)
    below = work_ref[...] + norm_backward(attn_in_grad, normed_one, inverse_one, gain_one)
    grad_out[...] = below
    row = lax.broadcasted_iota(jnp.int32, (MISC, width), 0)
    vectors = jnp.zeros((MISC, width), jnp.float32)
    for i, entry in enumerate(
        (first_gain_grad, first_bias_grad, second_gain_grad, second_bias_grad)
    ):
        vectors = jnp.where(row == experts + i, entry, vectors)
    weight_grad[:, 4 * width :] = (router_grad + vectors.T).astype(jnp.bfloat16)
    if not first:
        sent_ref[...] = send_grads(
            place_below, gates_of(gate_masks(chosen_below), probs_below[...]), below
        )


def attn_backward(kept, returned, back, grad, weight, below):
    last, first = below is not None, below is None
    state, qkv, mixed, middle, probs, chosen, pick = kept
    operands = [state, middle, qkv, mixed, probs, chosen, pick, returned, back, grad, weight]
    operands += [] if first else list(below)
    length, width = state.shape
    slots = returned.shape[0]
    outs = [
        jax.ShapeDtypeStruct((length, width), jnp.float32),
        jax.ShapeDtypeStruct(weight.shape, jnp.bfloat16),
    ]
    if last:
        outs.append(jax.ShapeDtypeStruct((length, width), jnp.float32))
    if not first:
        outs.append(jax.ShapeDtypeStruct((slots, width), jnp.bfloat16))
    return pl.pallas_call(
        functools.partial(attn_backward_kernel, last, first, slots // SLOTS),
        in_specs=whole(len(operands)),
        out_specs=whole(len(outs)),
        out_shape=outs,
        scratch_shapes=[
            pltpu.VMEM((length, width), jnp.bfloat16),
            pltpu.VMEM((length, 3 * width), jnp.bfloat16),
            pltpu.VMEM((length, width), jnp.float32),
        ],
        name="attn_backward",
    )(*operands)


def exchange(rows, experts):
    count, width = rows.shape
    moved = lax.all_to_all(
        rows.reshape(experts, count // experts, width),
        "expert",
        split_axis=0,
        concat_axis=0,
        tiled=True,
    )
    return moved.reshape(count, width)


def sum_over_experts(share, experts):
    count, width = share.shape
    parts = lax.all_to_all(
        share.reshape(experts, count // experts, width),
        "expert",
        split_axis=0,
        concat_axis=0,
        tiled=True,
    )
    total = jnp.sum(parts.astype(jnp.float32), axis=0).astype(jnp.bfloat16)
    spread = lax.all_to_all(
        jnp.broadcast_to(total[None], parts.shape),
        "expert",
        split_axis=0,
        concat_axis=0,
        tiled=True,
    )
    return spread.reshape(count, width).astype(jnp.float32)


def routing(chosen, experts):
    length = chosen.shape[0]
    masks = (chosen.T[:, :, None] == jnp.arange(experts, dtype=jnp.int32)).astype(jnp.bfloat16)
    named = masks[0] + masks[1]
    earlier = jnp.tril(jnp.ones((length, length), jnp.bfloat16), -1)
    before = matmul(earlier, named)
    slots = jnp.sum(before[None] * masks.astype(jnp.float32), axis=-1).astype(jnp.int32)
    position = chosen.T * SLOTS + slots
    every = jnp.arange(experts * SLOTS, dtype=jnp.int32)
    pick = (position[:, :, None] == every).astype(jnp.bfloat16)
    place = (position[:, None, :] == every[:, None]).astype(jnp.bfloat16)
    return pick, place


def unpack_attn(packed, width, experts):
    base = 4 * width
    vectors = packed[:, base + experts : base + experts + 4].T
    return (
        vectors[0],
        vectors[1],
        packed[:, : 3 * width],
        packed[:, 3 * width : base],
        vectors[2],
        vectors[3],
        packed[:, base : base + experts],
    )


def per_device(
    inputs,
    routes,
    first_gain,
    first_bias,
    qkv_weight,
    proj_weight,
    second_gain,
    second_bias,
    router_weight,
    hidden_weight,
    output_weight,
    cotangent,
):
    experts = lax.axis_size("expert")
    length, width = inputs.shape[1:]
    depth = routes.shape[0]
    attn_pack = [
        jnp.concatenate(
            [
                qkv_weight[layer],
                proj_weight[layer],
                router_weight[layer],
                first_gain[layer][:, None],
                first_bias[layer][:, None],
                second_gain[layer][:, None],
                second_bias[layer][:, None],
                jnp.zeros((qkv_weight.shape[1], MISC - experts - 4), jnp.bfloat16),
            ],
            axis=1,
        )
        for layer in range(routes.shape[0])
    ]
    expert_pack = [
        jnp.concatenate([hidden_weight[layer, 0].T, output_weight[layer, 0]], axis=1)
        for layer in range(routes.shape[0])
    ]
    depth = routes.shape[0]
    source = inputs[0]
    saved = []
    for layer in range(depth):
        last = layer == depth - 1
        weight = lax.all_gather(attn_pack[layer], "wshard", axis=0, tiled=True)
        chosen = routes[layer, 0]
        pick, place = routing(chosen, experts)
        state, qkv, mixed, middle, probs, sent = attn_forward(
            source, weight, chosen, place, cotangent[0] if last else None
        )
        received = exchange(sent, experts)
        expert_full = lax.all_gather(expert_pack[layer], "wshard", axis=0, tiled=True)
        if last:
            expert_grad, result, row_grad = ffn_both(received, expert_full)
            pre = None
        else:
            pre, result = ffn_forward(received, expert_full)
        returned = exchange(result, experts)
        source = (middle, returned, probs, chosen, pick)
        kept = (state, qkv, mixed, middle, probs, chosen, pick)
        saved.append((kept, weight, returned, received, pre, expert_full, place))
    grad = cotangent[0]
    layer_parts = []
    expert_parts = []
    share = None
    for layer in reversed(range(depth)):
        kept, weight, returned, received, pre, expert_full, _ = saved[layer]
        if layer < depth - 1:
            expert_grad, row_grad = ffn_backward(received, exchange(sent, experts), pre, expert_full)
        if share is not None:
            expert_grad, share = lax.optimization_barrier((expert_grad, share))
        expert_part = lax.psum_scatter(expert_grad, "wshard", scatter_dimension=0, tiled=True)
        below = None
        if layer > 0:
            kept_below, place_below = saved[layer - 1][0], saved[layer - 1][-1]
            below = (kept_below[4], kept_below[5], place_below)
        results = attn_backward(kept, returned, exchange(row_grad, experts), grad, weight, below)
        grad, attn_grad = results[:2]
        if layer == depth - 1:
            outputs = results[2]
        if layer > 0:
            sent = results[-1]
        attn_grad, expert_part = lax.optimization_barrier((attn_grad, expert_part))
        if share is not None:
            attn_grad, share = lax.optimization_barrier((attn_grad, share))
            layer_parts.append(unpack_attn(sum_over_experts(share, experts), width, experts))
        share = lax.psum_scatter(attn_grad, "wshard", scatter_dimension=0, tiled=True)
        expert_parts.append(
            (
                expert_part[:, :width].T.astype(jnp.float32),
                expert_part[:, width:].astype(jnp.float32),
            )
        )
    layer_parts.append(unpack_attn(sum_over_experts(share, experts), width, experts))
    layer_parts = list(reversed(layer_parts))
    expert_parts = list(reversed(expert_parts))
    stacked = [jnp.stack([entry[index] for entry in layer_parts]) for index in range(7)]
    hidden_grads = jnp.stack([entry[0] for entry in expert_parts])[:, None]
    output_grads = jnp.stack([entry[1] for entry in expert_parts])[:, None]
    return (
        outputs[None],
        grad[None],
        stacked[0],
        stacked[1],
        stacked[2],
        stacked[3],
        stacked[4],
        stacked[5],
        stacked[6],
        hidden_grads,
        output_grads,
    )


def solution(mesh):
    in_specs = (
        P(("expert", "wshard"), None, None),
        P(None, ("expert", "wshard"), None, None),
        P(None, "wshard"),
        P(None, "wshard"),
        P(None, "wshard", None),
        P(None, "wshard", None),
        P(None, "wshard"),
        P(None, "wshard"),
        P(None, "wshard", None),
        P(None, "expert", None, "wshard"),
        P(None, "expert", "wshard", None),
        P(("expert", "wshard"), None, None),
    )
    out_specs = (
        P(("expert", "wshard"), None, None),
        P(("expert", "wshard"), None, None),
        P(None, "wshard"),
        P(None, "wshard"),
        P(None, "wshard", None),
        P(None, "wshard", None),
        P(None, "wshard"),
        P(None, "wshard"),
        P(None, "wshard", None),
        P(None, "expert", None, "wshard"),
        P(None, "expert", "wshard", None),
    )
    return jax.shard_map(
        per_device, mesh=mesh, in_specs=in_specs, out_specs=out_specs, check_vma=False
    )
```

```python
import functools
import math

import jax
import jax.numpy as jnp
from jax import lax
from jax.experimental import pallas as pl
from jax.experimental.pallas import tpu as pltpu
from jax.sharding import PartitionSpec as P

HEADS = 12
SLOTS = 32
BLOCKS = 8
MISC = 128

EPSILON = 1e-06
ROOT_HALF = 0.7071067811865476
INV_ROOT_TAU = 0.3989422804014327


def standardize(rows):
    center = jnp.mean(rows, axis=-1, keepdims=True)
    shifted = rows - center
    variance = jnp.mean(shifted * shifted, axis=-1, keepdims=True)
    inverse = lax.rsqrt(variance + EPSILON)
    return (shifted * inverse, inverse)


def norm_backward(grad_in, normed, inverse, gain):
    scaled = grad_in * gain.astype(jnp.float32)
    first = jnp.mean(scaled, axis=-1, keepdims=True)
    second = jnp.mean(scaled * normed, axis=-1, keepdims=True)
    return inverse * (scaled - first - normed * second)


def matmul(left, right):
    return jnp.dot(left, right, preferred_element_type=jnp.float32)


def dot_nt(left, right):
    return lax.dot_general(
        left, right, (((1,), (1,)), ((), ())), preferred_element_type=jnp.float32
    )


def dot_tn(left, right):
    return lax.dot_general(
        left, right, (((0,), (0,)), ((), ())), preferred_element_type=jnp.float32
    )


def ffn_forward_kernel(rows_ref, weight_ref, pre_ref, out_ref, total):
    step = pl.program_id(0)
    width = rows_ref.shape[1]
    pre = dot_nt(rows_ref[...], weight_ref[:, :width])
    pre_ref[...] = pre
    act = (0.5 * pre * (1.0 + lax.erf(pre * ROOT_HALF))).astype(jnp.bfloat16)
    part = matmul(act, weight_ref[:, width:])

    @pl.when(step == 0)
    def _():
        total[...] = part

    @pl.when(step > 0)
    def _():
        total[...] += part

    @pl.when(step == pl.num_programs(0) - 1)
    def _():
        out_ref[...] = total[...].astype(out_ref.dtype)


def ffn_forward(rows, weight):
    count, width = rows.shape
    hidden = weight.shape[0]
    block = hidden // BLOCKS
    return pl.pallas_call(
        ffn_forward_kernel,
        grid=(BLOCKS,),
        in_specs=[
            pl.BlockSpec((count, width), lambda j: (0, 0)),
            pl.BlockSpec((block, 2 * width), lambda j: (j, 0)),
        ],
        out_specs=[
            pl.BlockSpec((count, block), lambda j: (0, j)),
            pl.BlockSpec((count, width), lambda j: (0, 0)),
        ],
        out_shape=[
            jax.ShapeDtypeStruct((count, hidden), jnp.float32),
            jax.ShapeDtypeStruct((count, width), jnp.bfloat16),
        ],
        scratch_shapes=[pltpu.VMEM((count, width), jnp.float32)],
        name="ffn_forward",
    )(rows, weight)


def ffn_backward_kernel(
    rows_ref, grads_ref, pre_ref, weight_ref, hidden_grad_ref, output_grad_ref, out_ref, total
):
    step = pl.program_id(0)
    width = rows_ref.shape[1]
    pre = pre_ref[...]
    phi = 0.5 * (1.0 + lax.erf(pre * ROOT_HALF))
    act = (pre * phi).astype(jnp.bfloat16)
    grads = grads_ref[...]
    act_grad = dot_nt(grads, weight_ref[:, width:])
    slope = phi + pre * jnp.exp(-0.5 * pre * pre) * INV_ROOT_TAU
    pre_grad = (act_grad * slope).astype(jnp.bfloat16)
    hidden_grad_ref[...] = dot_tn(pre_grad, rows_ref[...]).astype(jnp.bfloat16)
    output_grad_ref[...] = dot_tn(act, grads).astype(jnp.bfloat16)
    part = matmul(pre_grad, weight_ref[:, :width])

    @pl.when(step == 0)
    def _():
        total[...] = part

    @pl.when(step > 0)
    def _():
        total[...] += part

    @pl.when(step == pl.num_programs(0) - 1)
    def _():
        out_ref[...] = total[...].astype(out_ref.dtype)


def ffn_backward(rows, grads, pre, weight):
    count, width = rows.shape
    hidden = weight.shape[0]
    block = hidden // BLOCKS
    return pl.pallas_call(
        ffn_backward_kernel,
        grid=(BLOCKS,),
        in_specs=[
            pl.BlockSpec((count, width), lambda j: (0, 0)),
            pl.BlockSpec((count, width), lambda j: (0, 0)),
            pl.BlockSpec((count, block), lambda j: (0, j)),
            pl.BlockSpec((block, 2 * width), lambda j: (j, 0)),
        ],
        out_specs=[
            pl.BlockSpec((block, width), lambda j: (j, 0)),
            pl.BlockSpec((block, width), lambda j: (j, 0)),
            pl.BlockSpec((count, width), lambda j: (0, 0)),
        ],
        out_shape=[
            jax.ShapeDtypeStruct((hidden, width), jnp.bfloat16),
            jax.ShapeDtypeStruct((hidden, width), jnp.bfloat16),
            jax.ShapeDtypeStruct((count, width), jnp.bfloat16),
        ],
        scratch_shapes=[pltpu.VMEM((count, width), jnp.float32)],
        name="ffn_backward",
    )(rows, grads, pre, weight)


def ffn_both_kernel(rows_ref, grads_ref, weight_ref, weight_grad_ref, out_ref, back_ref, total, back):
    step = pl.program_id(0)
    width = rows_ref.shape[1]
    rows = rows_ref[...]
    grads = grads_ref[...]
    pre = dot_nt(rows, weight_ref[:, :width])
    act_grad = dot_nt(grads, weight_ref[:, width:])
    phi = 0.5 * (1.0 + lax.erf(pre * ROOT_HALF))
    act = (pre * phi).astype(jnp.bfloat16)
    slope = phi + pre * jnp.exp(-0.5 * pre * pre) * INV_ROOT_TAU
    pre_grad = (act_grad * slope).astype(jnp.bfloat16)
    part = matmul(act, weight_ref[:, width:])
    back_part = matmul(pre_grad, weight_ref[:, :width])
    weight_grad_ref[:, :width] = dot_tn(pre_grad, rows).astype(jnp.bfloat16)
    weight_grad_ref[:, width:] = dot_tn(act, grads).astype(jnp.bfloat16)

    @pl.when(step == 0)
    def _():
        total[...] = part
        back[...] = back_part

    @pl.when(step > 0)
    def _():
        total[...] += part
        back[...] += back_part

    @pl.when(step == pl.num_programs(0) - 1)
    def _():
        out_ref[...] = total[...].astype(out_ref.dtype)
        back_ref[...] = back[...].astype(back_ref.dtype)


def ffn_both(pairs, weight):
    count, width = pairs.shape[0], pairs.shape[1] // 2
    hidden = weight.shape[0]
    block = hidden // BLOCKS
    return pl.pallas_call(
        ffn_both_kernel,
        grid=(BLOCKS,),
        in_specs=[
            pl.BlockSpec((count, width), lambda j: (0, 0)),
            pl.BlockSpec((count, width), lambda j: (0, 1)),
            pl.BlockSpec((block, 2 * width), lambda j: (j, 0)),
        ],
        out_specs=[
            pl.BlockSpec((block, 2 * width), lambda j: (j, 0)),
            pl.BlockSpec((count, width), lambda j: (0, 0)),
            pl.BlockSpec((count, width), lambda j: (0, 0)),
        ],
        out_shape=[
            jax.ShapeDtypeStruct((hidden, 2 * width), jnp.bfloat16),
            jax.ShapeDtypeStruct((count, width), jnp.bfloat16),
            jax.ShapeDtypeStruct((count, width), jnp.bfloat16),
        ],
        scratch_shapes=[
            pltpu.VMEM((count, width), jnp.float32),
            pltpu.VMEM((count, width), jnp.float32),
        ],
        name="ffn_both",
    )(pairs, pairs, weight)


def lanes_of(shape):
    return lax.broadcasted_iota(jnp.int32, shape, len(shape) - 1)


def gate_masks(chosen_ref):
    length = chosen_ref.shape[0]
    lane = lanes_of((length, MISC))
    return [chosen_ref[:, k : k + 1] == lane for k in range(2)]


def gates_of(masks, probs):
    return [jnp.sum(jnp.where(mask, probs, 0.0), axis=-1, keepdims=True) for mask in masks]


def small_params(weight_ref, width, experts):
    flipped = weight_ref[:, 4 * width :].astype(jnp.float32).T
    return [flipped[experts + i : experts + i + 1, :] for i in range(4)]


def blocked(count, body):
    lax.fori_loop(0, count, lambda i, carry: (body(i), carry)[1], 0)


def block_of(i, size):
    return pl.ds(pl.multiple_of(i * size, size), size)


def send_grads(place_ref, gates, grad):
    total = None
    for k in range(2):
        part = matmul(place_ref[k], (gates[k] * grad).astype(jnp.bfloat16))
        total = part if total is None else total + part
    return total.astype(jnp.bfloat16)


def attn_forward_kernel(first, last, experts, *refs):
    refs = list(refs)
    if first:
        state_in = refs.pop(0)
    else:
        middle_in, returned_ref, probs_in, chosen_in, pick_ref = refs[:5]
        refs = refs[5:]
    weight_ref, chosen_ref, place_ref = refs[:3]
    refs = refs[3:]
    if last:
        grad_ref = refs.pop(0)
    if not first:
        state_out = refs.pop(0)
    qkv_ref, mixed_ref, middle_ref, probs_ref, sent_ref = refs
    width = weight_ref.shape[0]
    scale = 1.0 / math.sqrt(width // HEADS)
    if first:
        state = state_in[...]
    else:
        gates = gates_of(gate_masks(chosen_in), probs_in[...])
        returned = returned_ref[...]
        state = middle_in[...]
        added = [gates[k] * matmul(pick_ref[k], returned) for k in range(2)]
        state = state + (added[0] + added[1])
        state_out[...] = state
    gain_one, bias_one, gain_two, bias_two = small_params(weight_ref, width, experts)
    normed, _ = standardize(state)
    attn_in = (normed * gain_one + bias_one).astype(jnp.bfloat16)

    def project(i):
        cols = block_of(i, 384)
        qkv_ref[:, cols] = matmul(attn_in, weight_ref[:, cols]).astype(jnp.bfloat16)

    blocked(3 * width // 384, project)
    length = state.shape[0]
    half = lanes_of((length, 128)) < 64

    def heads(i):
        query = qkv_ref[:, block_of(i, 128)]
        keys = qkv_ref[:, pl.ds(pl.multiple_of(width + i * 128, 128), 128)]
        values = qkv_ref[:, pl.ds(pl.multiple_of(2 * width + i * 128, 128), 128)]
        out = []
        for side in range(2):
            mine = half if side == 0 else jnp.logical_not(half)
            scores = dot_nt(jnp.where(mine, query, jnp.zeros_like(query)), keys) * scale
            log_total = jnp.log(jnp.sum(jnp.exp(scores), axis=-1, keepdims=True))
            probs_low = jnp.exp(scores - log_total).astype(jnp.bfloat16)
            out.append(matmul(probs_low, values))
        mixed_ref[:, block_of(i, 128)] = jnp.where(half, out[0], out[1]).astype(jnp.bfloat16)

    blocked(HEADS // 2, heads)
    mixed = mixed_ref[...]

    def combine(i):
        cols = block_of(i, 384)
        middle_ref[:, cols] = matmul(
            mixed, weight_ref[:, pl.ds(pl.multiple_of(3 * width + i * 384, 384), 384)]
        )

    blocked(width // 384, combine)
    middle = state + middle_ref[...]
    middle_ref[...] = middle
    normed_two, _ = standardize(middle)
    moe_in = (normed_two * gain_two + bias_two).astype(jnp.bfloat16)
    logits = matmul(moe_in, weight_ref[:, 4 * width :])
    raised = jnp.where(lanes_of(logits.shape) < experts, jnp.exp(logits), 0.0)
    probs = raised / jnp.sum(raised, axis=-1, keepdims=True)
    probs_ref[...] = probs
    sent = matmul(place_ref[0] + place_ref[1], moe_in)
    sent_ref[:, :width] = sent.astype(jnp.bfloat16)
    if last:
        sent_ref[:, width:] = send_grads(
            place_ref, gates_of(gate_masks(chosen_ref), probs), grad_ref[...]
        )


def whole(count):
    return [pl.BlockSpec(memory_space=pltpu.VMEM) for _ in range(count)]


def attn_forward(source, weight, chosen, place, cotangent):
    first, last = not isinstance(source, tuple), cotangent is not None
    operands = [source] if first else list(source)
    length, width = operands[0].shape
    slots = place.shape[1]
    operands += [weight, chosen, place] + ([cotangent] if last else [])
    outs = [] if first else [jax.ShapeDtypeStruct((length, width), jnp.float32)]
    outs += [
        jax.ShapeDtypeStruct((length, 3 * width), jnp.bfloat16),
        jax.ShapeDtypeStruct((length, width), jnp.bfloat16),
        jax.ShapeDtypeStruct((length, width), jnp.float32),
        jax.ShapeDtypeStruct((length, MISC), jnp.float32),
        jax.ShapeDtypeStruct((slots, width * (2 if last else 1)), jnp.bfloat16),
    ]
    results = pl.pallas_call(
        functools.partial(attn_forward_kernel, first, last, slots // SLOTS),
        in_specs=whole(len(operands)),
        out_specs=whole(len(outs)),
        out_shape=outs,
        name="attn_forward",
    )(*operands)
    return ([source] if first else []) + list(results)


def attn_backward_kernel(last, first, experts, *refs):
    refs = list(refs)
    (
        state_ref,
        middle_ref,
        qkv_ref,
        mixed_ref,
        probs_ref,
        chosen_ref,
        pick_ref,
        returned_ref,
        back_ref,
        grad_ref,
        weight_ref,
    ) = refs[:11]
    refs = refs[11:]
    if not first:
        probs_below, chosen_below, place_below = refs[:3]
        refs = refs[3:]
    grad_out, weight_grad = refs[:2]
    refs = refs[2:]
    if last:
        output_ref = refs.pop(0)
    if not first:
        sent_ref = refs.pop(0)
    mixed_grad_ref, qkv_grad_ref, work_ref = refs
    width = weight_ref.shape[0]
    scale = 1.0 / math.sqrt(width // HEADS)
    grad = grad_ref[...]
    length = grad.shape[0]
    gain_one, bias_one, gain_two, bias_two = small_params(weight_ref, width, experts)
    masks = gate_masks(chosen_ref)
    probs = probs_ref[...]
    middle = middle_ref[...]
    gates = gates_of(masks, probs)
    returned = returned_ref[...]
    picked = [matmul(pick_ref[k], returned) for k in range(2)]
    if last:
        output_ref[...] = middle + (gates[0] * picked[0] + gates[1] * picked[1])
    prob_grad = jnp.zeros_like(probs)
    for k in range(2):
        gate_grad = jnp.sum(grad * picked[k], axis=-1, keepdims=True)
        prob_grad = prob_grad + jnp.where(masks[k], gate_grad, 0.0)
    logit_grad = (
        probs * (prob_grad - jnp.sum(probs * prob_grad, axis=-1, keepdims=True))
    ).astype(jnp.bfloat16)
    normed_two, inverse_two = standardize(middle)
    moe_in = (normed_two * gain_two + bias_two).astype(jnp.bfloat16)
    router_grad = dot_tn(moe_in, logit_grad)
    moe_in_grad = matmul(pick_ref[0] + pick_ref[1], back_ref[...]) + dot_nt(
        logit_grad, weight_ref[:, 4 * width :]
    )
    second_gain_grad = jnp.sum(moe_in_grad * normed_two, axis=0, keepdims=True)
    second_bias_grad = jnp.sum(moe_in_grad, axis=0, keepdims=True)
    middle_grad = grad + norm_backward(moe_in_grad, normed_two, inverse_two, gain_two)
    work_ref[...] = middle_grad
    middle_low = middle_grad.astype(jnp.bfloat16)
    weight_grad[:, 3 * width : 4 * width] = dot_tn(mixed_ref[...], middle_low).astype(jnp.bfloat16)
    mixed_grad_ref[...] = dot_nt(middle_low, weight_ref[:, 3 * width : 4 * width]).astype(
        jnp.bfloat16
    )
    half = lanes_of((length, 128)) < 64

    def heads(i):
        query_cols = block_of(i, 128)
        keys_cols = pl.ds(pl.multiple_of(width + i * 128, 128), 128)
        values_cols = pl.ds(pl.multiple_of(2 * width + i * 128, 128), 128)
        query, keys, values = qkv_ref[:, query_cols], qkv_ref[:, keys_cols], qkv_ref[:, values_cols]
        mixed_grad = mixed_grad_ref[:, query_cols]
        parts = []
        for side in range(2):
            mine = half if side == 0 else jnp.logical_not(half)
            scores = dot_nt(jnp.where(mine, query, jnp.zeros_like(query)), keys) * scale
            log_total = jnp.log(jnp.sum(jnp.exp(scores), axis=-1, keepdims=True))
            probs_att = jnp.exp(scores - log_total)
            prob_grad_att = dot_nt(jnp.where(mine, mixed_grad, jnp.zeros_like(mixed_grad)), values)
            row_total = jnp.sum(probs_att * prob_grad_att, axis=-1, keepdims=True)
            score_low = (probs_att * (prob_grad_att - row_total) * scale).astype(jnp.bfloat16)
            parts.append(
                (
                    matmul(score_low, keys),
                    dot_tn(score_low, query),
                    dot_tn(probs_att.astype(jnp.bfloat16), mixed_grad),
                )
            )
        for cols, index in ((query_cols, 0), (keys_cols, 1), (values_cols, 2)):
            qkv_grad_ref[:, cols] = jnp.where(half, parts[0][index], parts[1][index]).astype(
                jnp.bfloat16
            )

    blocked(HEADS // 2, heads)
    normed_one, inverse_one = standardize(state_ref[...])
    attn_in = (normed_one * gain_one + bias_one).astype(jnp.bfloat16)

    def weights(i):
        cols = block_of(i, 384)
        weight_grad[:, cols] = dot_tn(attn_in, qkv_grad_ref[:, cols]).astype(jnp.bfloat16)

    blocked(3 * width // 384, weights)
    attn_in_grad = dot_nt(qkv_grad_ref[...], weight_ref[:, : 3 * width])
    first_gain_grad = jnp.sum(attn_in_grad * normed_one, axis=0, keepdims=True)
    first_bias_grad = jnp.sum(attn_in_grad, axis=0, keepdims=True)
    below = work_ref[...] + norm_backward(attn_in_grad, normed_one, inverse_one, gain_one)
    grad_out[...] = below
    row = lax.broadcasted_iota(jnp.int32, (MISC, width), 0)
    vectors = jnp.zeros((MISC, width), jnp.float32)
    for i, entry in enumerate(
        (first_gain_grad, first_bias_grad, second_gain_grad, second_bias_grad)
    ):
        vectors = jnp.where(row == experts + i, entry, vectors)
    weight_grad[:, 4 * width :] = (router_grad + vectors.T).astype(jnp.bfloat16)
    if not first:
        sent_ref[...] = send_grads(
            place_below, gates_of(gate_masks(chosen_below), probs_below[...]), below
        )


def attn_backward(kept, returned, back, grad, weight, below):
    last, first = below is not None, below is None
    state, qkv, mixed, middle, probs, chosen, pick = kept
    operands = [state, middle, qkv, mixed, probs, chosen, pick, returned, back, grad, weight]
    operands += [] if first else list(below)
    length, width = state.shape
    slots = returned.shape[0]
    outs = [
        jax.ShapeDtypeStruct((length, width), jnp.float32),
        jax.ShapeDtypeStruct(weight.shape, jnp.bfloat16),
    ]
    if last:
        outs.append(jax.ShapeDtypeStruct((length, width), jnp.float32))
    if not first:
        outs.append(jax.ShapeDtypeStruct((slots, width), jnp.bfloat16))
    return pl.pallas_call(
        functools.partial(attn_backward_kernel, last, first, slots // SLOTS),
        in_specs=whole(len(operands)),
        out_specs=whole(len(outs)),
        out_shape=outs,
        scratch_shapes=[
            pltpu.VMEM((length, width), jnp.bfloat16),
            pltpu.VMEM((length, 3 * width), jnp.bfloat16),
            pltpu.VMEM((length, width), jnp.float32),
        ],
        name="attn_backward",
    )(*operands)


def exchange(rows, experts):
    count, width = rows.shape
    moved = lax.all_to_all(
        rows.reshape(experts, count // experts, width),
        "expert",
        split_axis=0,
        concat_axis=0,
        tiled=True,
    )
    return moved.reshape(count, width)


def sum_over_experts(share, experts):
    count, width = share.shape
    parts = lax.all_to_all(
        share.reshape(experts, count // experts, width),
        "expert",
        split_axis=0,
        concat_axis=0,
        tiled=True,
    )
    total = jnp.sum(parts.astype(jnp.float32), axis=0).astype(jnp.bfloat16)
    spread = lax.all_to_all(
        jnp.broadcast_to(total[None], parts.shape),
        "expert",
        split_axis=0,
        concat_axis=0,
        tiled=True,
    )
    return spread.reshape(count, width).astype(jnp.float32)


def routing(chosen, experts):
    length = chosen.shape[0]
    masks = (chosen.T[:, :, None] == jnp.arange(experts, dtype=jnp.int32)).astype(jnp.bfloat16)
    named = masks[0] + masks[1]
    earlier = jnp.tril(jnp.ones((length, length), jnp.bfloat16), -1)
    before = matmul(earlier, named)
    slots = jnp.sum(before[None] * masks.astype(jnp.float32), axis=-1).astype(jnp.int32)
    position = chosen.T * SLOTS + slots
    every = jnp.arange(experts * SLOTS, dtype=jnp.int32)
    pick = (position[:, :, None] == every).astype(jnp.bfloat16)
    place = (position[:, None, :] == every[:, None]).astype(jnp.bfloat16)
    return pick, place


def unpack_attn(packed, width, experts):
    base = 4 * width
    vectors = packed[:, base + experts : base + experts + 4].T
    return (
        vectors[0],
        vectors[1],
        packed[:, : 3 * width],
        packed[:, 3 * width : base],
        vectors[2],
        vectors[3],
        packed[:, base : base + experts],
    )


def per_device(
    inputs,
    routes,
    first_gain,
    first_bias,
    qkv_weight,
    proj_weight,
    second_gain,
    second_bias,
    router_weight,
    hidden_weight,
    output_weight,
    cotangent,
):
    experts = lax.axis_size("expert")
    length, width = inputs.shape[1:]
    depth = routes.shape[0]
    attn_pack = [
        jnp.concatenate(
            [
                qkv_weight[layer],
                proj_weight[layer],
                router_weight[layer],
                first_gain[layer][:, None],
                first_bias[layer][:, None],
                second_gain[layer][:, None],
                second_bias[layer][:, None],
                jnp.zeros((qkv_weight.shape[1], MISC - experts - 4), jnp.bfloat16),
            ],
            axis=1,
        )
        for layer in range(routes.shape[0])
    ]
    expert_pack = [
        jnp.concatenate([hidden_weight[layer, 0].T, output_weight[layer, 0]], axis=1)
        for layer in range(routes.shape[0])
    ]
    depth = routes.shape[0]
    source = inputs[0]
    saved = []
    for layer in range(depth):
        last = layer == depth - 1
        weight = lax.all_gather(attn_pack[layer], "wshard", axis=0, tiled=True)
        chosen = routes[layer, 0]
        pick, place = routing(chosen, experts)
        state, qkv, mixed, middle, probs, sent = attn_forward(
            source, weight, chosen, place, cotangent[0] if last else None
        )
        received = exchange(sent, experts)
        expert_full = lax.all_gather(expert_pack[layer], "wshard", axis=0, tiled=True)
        if last:
            expert_grad, result, row_grad = ffn_both(received, expert_full)
            pre = None
        else:
            pre, result = ffn_forward(received, expert_full)
        returned = exchange(result, experts)
        source = (middle, returned, probs, chosen, pick)
        kept = (state, qkv, mixed, middle, probs, chosen, pick)
        saved.append((kept, weight, returned, received, pre, expert_full, place))
    grad = cotangent[0]
    layer_parts = []
    expert_parts = []
    share = None
    for layer in reversed(range(depth)):
        kept, weight, returned, received, pre, expert_full, _ = saved[layer]
        if layer < depth - 1:
            expert_grad, output_grad, row_grad = ffn_backward(
                received, exchange(sent, experts), pre, expert_full
            )
        if share is not None:
            expert_grad, share = lax.optimization_barrier((expert_grad, share))
        expert_part = lax.psum_scatter(expert_grad, "wshard", scatter_dimension=0, tiled=True)
        below = None
        if layer > 0:
            kept_below, place_below = saved[layer - 1][0], saved[layer - 1][-1]
            below = (kept_below[4], kept_below[5], place_below)
        results = attn_backward(kept, returned, exchange(row_grad, experts), grad, weight, below)
        grad, attn_grad = results[:2]
        if layer == depth - 1:
            outputs = results[2]
        if layer > 0:
            sent = results[-1]
        attn_grad, expert_part = lax.optimization_barrier((attn_grad, expert_part))
        if share is not None:
            attn_grad, share = lax.optimization_barrier((attn_grad, share))
            layer_parts.append(unpack_attn(sum_over_experts(share, experts), width, experts))
        share = lax.psum_scatter(attn_grad, "wshard", scatter_dimension=0, tiled=True)
        if layer < depth - 1:
            output_grad, share = lax.optimization_barrier((output_grad, share))
            output_part = lax.psum_scatter(
                output_grad, "wshard", scatter_dimension=0, tiled=True
            )
        else:
            output_part = expert_part[:, width:]
        expert_parts.append(
            (
                expert_part[:, :width].T.astype(jnp.float32),
                output_part.astype(jnp.float32),
            )
        )
    layer_parts.append(unpack_attn(sum_over_experts(share, experts), width, experts))
    layer_parts = list(reversed(layer_parts))
    expert_parts = list(reversed(expert_parts))
    stacked = [jnp.stack([entry[index] for entry in layer_parts]) for index in range(7)]
    hidden_grads = jnp.stack([entry[0] for entry in expert_parts])[:, None]
    output_grads = jnp.stack([entry[1] for entry in expert_parts])[:, None]
    return (
        outputs[None],
        grad[None],
        stacked[0],
        stacked[1],
        stacked[2],
        stacked[3],
        stacked[4],
        stacked[5],
        stacked[6],
        hidden_grads,
        output_grads,
    )


def solution(mesh):
    in_specs = (
        P(("expert", "wshard"), None, None),
        P(None, ("expert", "wshard"), None, None),
        P(None, "wshard"),
        P(None, "wshard"),
        P(None, "wshard", None),
        P(None, "wshard", None),
        P(None, "wshard"),
        P(None, "wshard"),
        P(None, "wshard", None),
        P(None, "expert", None, "wshard"),
        P(None, "expert", "wshard", None),
        P(("expert", "wshard"), None, None),
    )
    out_specs = (
        P(("expert", "wshard"), None, None),
        P(("expert", "wshard"), None, None),
        P(None, "wshard"),
        P(None, "wshard"),
        P(None, "wshard", None),
        P(None, "wshard", None),
        P(None, "wshard"),
        P(None, "wshard"),
        P(None, "wshard", None),
        P(None, "expert", None, "wshard"),
        P(None, "expert", "wshard", None),
    )
    return jax.shard_map(
        per_device, mesh=mesh, in_specs=in_specs, out_specs=out_specs, check_vma=False
    )
```
